256 devices in a mesh: dp: 32 (over x, z_hi, core), ctx: 8 (over z_lo, y).
Axes of the slice: x: 4, y: 4, z: 8 (z_hi: 4, z_lo: 2; z = z_hi * 2 + z_lo), core: 2. Of those that a mesh axis runs over, the one named last changes fastest.
Arguments:
- hidden_in: bfloat16 [32, 1024, 2688], P('dp', 'ctx'), may hold values from -0.08984375 to 0.08984375
- queries: bfloat16 [32, 1024, 2048], P('dp', 'ctx'), may hold values from -60 to 60
- key_states: bfloat16 [32, 1024, 1024], P('dp', 'ctx'), may hold values from -4 to 4
- value_states: bfloat16 [32, 1024, 1024], P('dp', 'ctx'), may hold values from -6 to 6
- out_grad: bfloat16 [32, 1024, 2048], P('dp', 'ctx'), may hold values from -48 to 48
- segment_ids: int32 [32, 1024], P('dp', 'ctx'), may hold values from 0 to 3, never falling along the last dimension, each value on 1 to 512 neighbouring positions
Outputs:
- query_grad: bfloat16 [32, 1024, 2048], P('dp', 'ctx')
- key_grad: bfloat16 [32, 1024, 1024], P('dp', 'ctx')
- value_grad: bfloat16 [32, 1024, 1024], P('dp', 'ctx')
- weight_grad: float32 [2688, 2048], P('dp', 'ctx')
The draws below stay inside these ranges and needn't reach their ends.
Inputs may be any that keep to these rules, and one draw needn't show every extreme that they name: `segment_ids`: documents of a trace are numbered in order of position.
All inputs are finite; a program needn't handle non-finite values.
Results may differ from the reference program's by a relative error of at most 0.0096.
Values may be sent and summed in bfloat16 or wider, within the bound.
A program may use at most 128 MiB of HBM per device.

```python
import math
import jax
import jax.numpy as jnp
import numpy as np
from jax import lax

QH = 16
KVH = 8
HD = 128
DW = 2688
WIN = 1024
SEGS = 4
TOK_DEV = 128
SEQ = 1024
TRACES = 32
HOPS = 7


def draw_pair(key):
    base_key = jax.random.fold_in(key, 4242)
    query_key, keys_key = jax.random.split(base_key, 2)
    query_shape = (TRACES, SEQ, QH * HD)
    key_shape = (TRACES, SEQ, KVH * HD)
    query_vals = jnp.clip(jax.random.normal(query_key, query_shape, jnp.float32), -4.0, 4.0)
    key_vals = jnp.clip(jax.random.normal(keys_key, key_shape, jnp.float32), -4.0, 4.0)
    return (query_vals, key_vals)


def draw_queries(key, part):
    return draw_pair(key)[0].astype(jnp.bfloat16)


def draw_key_states(key, part):
    return draw_pair(key)[1].astype(jnp.bfloat16)


def with_spikes(result, stream_key, source, target, shards_of, factor):
    def block_of(position):
        return (jnp.arange(result.shape[position]) // (result.shape[position] // shards_of)).reshape((-1,) + (1,) * (result.ndim - 1 - position))

    one_side = jax.random.permutation(stream_key, shards_of)[block_of(target)]
    other_side = (block_of(target) + shards_of // 2) % shards_of
    return jnp.where((block_of(source) == one_side) | (block_of(source) == other_side), factor * result, result)


def shard_levels(key, dims, pieces, smallest, high):
    def one(dim, parts):
        draws = jax.random.uniform(jax.random.fold_in(jax.random.fold_in(key, 6), dim), (parts,), jnp.float32, smallest / len(pieces), high / len(pieces))
        return jnp.repeat(jnp.exp(draws), dims[dim] // parts).reshape((-1,) + (1,) * (len(dims) - dim - 1))

    factor_of = one(*pieces[0])
    for cut in pieces[1:]:
        factor_of = factor_of * one(*cut)
    return factor_of


def split_up(count, total, limit, slope):
    portions = [(1 << 20) // math.isqrt(standing ** slope) + 1 for standing in range(2, count + 1)]
    spare, counts = total - limit - (count - 1), [1] * (count - 1)
    while spare > 0:
        free = [i for i in range(count - 1) if counts[i] < limit]
        mass, remaining = sum([portions[i] for i in free]), spare
        for i in free:
            extra = min(limit - counts[i], max(1, remaining * portions[i] // mass), spare)
            counts[i] = counts[i] + extra
            spare = spare - extra
    return np.array([limit] + counts)


def uneven_parts(rng, count, total, reach, lean):
    if count == 2:
        one = jax.random.randint(rng, (), max(1, total - reach), min(reach, total - 1) + 1)
        return jnp.stack([one, total - one])
    sizes = jnp.asarray(split_up(count, total, reach, lean), jnp.int32)
    twos = (count - 1) // 2
    donor, receiver = sizes[1:1 + 2 * twos:2], sizes[2:2 + 2 * twos:2]
    margin = jnp.minimum(donor - 1, reach - receiver)
    moved = jax.random.randint(jax.random.fold_in(rng, 1), (twos,), 0, 1 << 20) % (margin + 1)
    sizes = sizes.at[1:1 + 2 * twos:2].set(donor - moved).at[2:2 + 2 * twos:2].set(receiver + moved)
    return sizes[jax.random.permutation(jax.random.fold_in(rng, 2), count)]


def noise(own_key, shape, deviation, limit, pieces=(), kind=jnp.bfloat16):
    level = shard_levels(own_key, shape, pieces, -0.22, 0.18) if pieces else 1.0
    values = jax.random.normal(own_key, shape, jnp.float32) * deviation * level
    return jnp.minimum(jnp.maximum(values, -limit), limit).astype(kind)


def bell_draw_with(stream_key, dims, deviation, limit, shards, heavy, kind=jnp.bfloat16):
    drawn = deviation * jax.random.normal(stream_key, dims, jnp.float32)
    if shards:
        drawn = drawn * shard_levels(stream_key, dims, shards, -0.22, 0.18)
    return jnp.clip(with_spikes(drawn, jax.random.fold_in(stream_key, 3), *heavy), -limit, limit).astype(kind)


def setup_inputs(seed: int = 0) -> dict:
    keys = jax.random.split(jax.random.key(seed), 7)
    hidden_in = bell_draw_with(keys[0], (TRACES, SEQ, DW), 0.015, 0.08984375, ((0, 32), (1, 8)), (0, 2, 32, 2.75))
    queries = draw_queries(jax.random.fold_in(keys[6], 71), 0)
    key_states = draw_key_states(jax.random.fold_in(keys[6], 71), 0)
    value_states = noise(keys[3], (TRACES, SEQ, KVH * HD), 1.0, 6.0, ((0, 32), (1, 8)))
    out_grad = noise(keys[4], (TRACES, SEQ, QH * HD), 8.0, 48.0, ((0, 32), (1, 8)))
    segment_ids = jax.vmap(lambda own: jnp.searchsorted(jnp.cumsum(uneven_parts(own, SEGS, SEQ, SEQ // 2, 1)), jnp.arange(SEQ), side="right"))(jax.random.split(keys[5], TRACES)).reshape((TRACES, SEQ)).astype(jnp.int32)
    return {"hidden_in": hidden_in, "queries": queries, "key_states": key_states, "value_states": value_states, "out_grad": out_grad, "segment_ids": segment_ids}


SCORE_FLOOR = -1e30


def round_keep(values_in):
    return lax.optimization_barrier(values_in.astype(jnp.bfloat16)).astype(jnp.float32)


def one_trace(queries, key_states, value_states, out_grad, segment_ids):
    score_scale = HD ** -0.5
    group_size = QH // KVH
    rim_span = HOPS * TOK_DEV
    key_span = rim_span + TOK_DEV
    keys_padded = jnp.pad(key_states, ((rim_span, 0), (0, 0)))
    values_padded = jnp.pad(value_states, ((rim_span, 0), (0, 0)))
    segs_padded = jnp.pad(segment_ids, (rim_span, 0), constant_values=-1)

    def block_step(carried, block_index):
        key_total, value_total = carried
        first_row = (block_index * TOK_DEV).astype(jnp.int32)
        query_block = lax.dynamic_slice_in_dim(queries, first_row, TOK_DEV, 0).reshape(TOK_DEV, KVH, group_size, HD).astype(jnp.float32)
        grad_block = lax.dynamic_slice_in_dim(out_grad, first_row, TOK_DEV, 0).reshape(TOK_DEV, KVH, group_size, HD).astype(jnp.float32)
        key_block = lax.dynamic_slice_in_dim(keys_padded, first_row, key_span, 0).reshape(key_span, KVH, HD).astype(jnp.float32)
        value_block = lax.dynamic_slice_in_dim(values_padded, first_row, key_span, 0).reshape(key_span, KVH, HD).astype(jnp.float32)
        query_segs = lax.dynamic_slice_in_dim(segment_ids, first_row, TOK_DEV, 0)
        key_segs = lax.dynamic_slice_in_dim(segs_padded, first_row, key_span, 0)
        query_pos = first_row + jnp.arange(TOK_DEV, dtype=jnp.int32)
        key_pos = first_row - rim_span + jnp.arange(key_span, dtype=jnp.int32)
        distance = query_pos[:, None] - key_pos[None, :]
        allowed = (key_pos[None, :] >= 0) & (distance >= 0) & (distance < WIN) & (query_segs[:, None] == key_segs[None, :])
        scores = jnp.einsum("ikgd,jkd->kgij", query_block, key_block) * score_scale
        scores = jnp.where(allowed[None, None], scores, SCORE_FLOOR)
        row_peak = jnp.max(scores, axis=3, keepdims=True)
        weights = jnp.where(allowed[None, None], jnp.exp(scores - row_peak), 0.0)
        probs_full = weights / jnp.sum(weights, axis=3, keepdims=True)
        probs_low = round_keep(probs_full)
        attn_out = jnp.einsum("kgij,jkd->kgid", probs_low, value_block)
        row_delta = jnp.einsum("ikgd,kgid->kgi", grad_block, attn_out)
        dprobs = jnp.einsum("ikgd,jkd->kgij", grad_block, value_block)
        dscores = round_keep(probs_full * (dprobs - row_delta[..., None]))
        query_part = (jnp.einsum("kgij,jkd->ikgd", dscores, key_block) * score_scale).astype(jnp.bfloat16)
        key_part = round_keep(jnp.einsum("kgij,ikgd->jkd", dscores, query_block) * score_scale).reshape(key_span, KVH * HD)
        value_part = round_keep(jnp.einsum("kgij,ikgd->jkd", probs_low, grad_block)).reshape(key_span, KVH * HD)
        key_total = lax.dynamic_update_slice_in_dim(key_total, lax.dynamic_slice_in_dim(key_total, first_row, key_span, 0) + key_part, first_row, 0)
        value_total = lax.dynamic_update_slice_in_dim(value_total, lax.dynamic_slice_in_dim(value_total, first_row, key_span, 0) + value_part, first_row, 0)
        return (key_total, value_total), query_part.reshape(TOK_DEV, QH * HD)

    zeros_init = jnp.zeros((SEQ + rim_span, KVH * HD), jnp.float32)
    (key_total, value_total), query_blocks = lax.scan(block_step, (zeros_init, zeros_init), jnp.arange(SEQ // TOK_DEV, dtype=jnp.int32))
    key_grad = key_total[rim_span:].astype(jnp.bfloat16)
    value_grad = value_total[rim_span:].astype(jnp.bfloat16)
    return query_blocks.reshape(SEQ, QH * HD), key_grad, value_grad


def reference(hidden_in, queries, key_states, value_states, out_grad, segment_ids):
    def trace_step(grad_total, items):
        features, query_one, key_one, value_one, grad_one, segs_one = items
        query_grad, key_grad, value_grad = one_trace(query_one, key_one, value_one, grad_one, segs_one)
        both_grads = jnp.concatenate([key_grad, value_grad], axis=1)
        grad_total = grad_total + jnp.dot(features.T, both_grads, preferred_element_type=jnp.float32)
        return grad_total, (query_grad, key_grad, value_grad)

    start_total = jnp.zeros((DW, 2 * KVH * HD), jnp.float32)
    weight_grad, outputs = lax.scan(trace_step, start_total, (hidden_in, queries, key_states, value_states, out_grad, segment_ids))
    return outputs[0], outputs[1], outputs[2], weight_grad
```

```python
import functools

import jax
import jax.numpy as jnp
from jax import lax
from jax.experimental import pallas as pl
from jax.experimental.pallas import tpu as pltpu
from jax.sharding import PartitionSpec as P

HD = 128
TOK = 128
CTX = 8
NY = 4
NX = 4
NZ = 4
NC = 2
SPAN = 4
FLOOR = -1e30
SCALE = HD ** (-0.5)
EXP2_SCALE = SCALE * 1.4426950408889634
MESH = pl.DeviceIdType.MESH
F32 = jnp.float32
BF16 = jnp.bfloat16
PEERS = ((1, 2), (0, 2), (1, 1), (1, 3), (0, 1), (0, 3), (1, 0))
NT = (((1,), (1,)), ((), ()))
TN = (((0,), (0,)), ((), ()))


def dot(lhs, rhs, dims=(((1,), (0,)), ((), ()))):
    return lax.dot_general(lhs, rhs, dims, preferred_element_type=F32)


def kernel(
    h, q, k, v, do, seg, dq_out, dk_out, dv_out, w_out,
    hv, qs, dos, ks, vs, segs, segc, dqs, g4, dka, dva, hs, hall,
    wown, csend, crecv, xsend, xrecv, tsum, zsend, zrecv,
    lsem, asend, arecv, osend, orecv, gsend, grecv, hsend, hrecv,
    csem, crsem, xsem, xrsem, zsem, zrsem,
):
    feats = h.shape[1]
    half = feats // 2
    xrows = half // NX
    frows = w_out.shape[0]
    zrows = zsend.shape[1]
    dp = lax.axis_index("dp")
    ctx = lax.axis_index("ctx")
    x = dp // (NZ * NC)
    zh = (dp // NC) % NZ
    core = dp % NC
    zl = ctx // NY
    y = ctx % NY
    other = (zl + 1) % 2
    head = 2 * y + zl
    partner = other * NY + y

    def at(place, width):
        return pl.ds(pl.multiple_of(place * width, width), width)

    def place(nx, nz, nc, nl, ny):
        return ((nx * NZ + nz) * NC + nc, nl * NY + ny)

    def remote(src, dst, ssem, rsem, device):
        return pltpu.make_async_remote_copy(
            src_ref=src, dst_ref=dst, send_sem=ssem, recv_sem=rsem,
            device_id=device, device_id_type=MESH,
        )

    barrier = pltpu.get_barrier_semaphore()
    count = 0
    for dz in range(NZ):
        for dc in range(NC):
            for dl in range(2):
                if dz + dc + dl:
                    pl.semaphore_signal(
                        barrier, inc=1, device_id_type=MESH,
                        device_id=place(x, (zh + dz) % NZ, (core + dc) % NC, (zl + dl) % 2, y),
                    )
                    count += 1
    for dl in range(2):
        for dy in range(1, NY):
            pl.semaphore_signal(
                barrier, inc=1, device_id_type=MESH,
                device_id=place(x, zh, core, (zl + dl) % 2, (y + dy) % NY),
            )
            count += 1
    for dx in range(1, NX):
        pl.semaphore_signal(
            barrier, inc=1, device_id_type=MESH,
            device_id=place((x + dx) % NX, zh, core, zl, y),
        )
        count += 1

    own = at(ctx, TOK)
    local_in = [
        pltpu.make_async_copy(h, hv, lsem.at[0]),
        pltpu.make_async_copy(q.at[:, at(head, 2 * HD)], qs.at[own, :], lsem.at[1]),
        pltpu.make_async_copy(do.at[:, at(head, 2 * HD)], dos.at[own, :], lsem.at[2]),
        pltpu.make_async_copy(k.at[:, at(head, HD)], ks.at[own, :], lsem.at[3]),
        pltpu.make_async_copy(v.at[:, at(head, HD)], vs.at[own, :], lsem.at[4]),
        pltpu.make_async_copy(seg, segs.at[ctx], lsem.at[5]),
    ]
    for copy in local_in:
        copy.start()
    pl.semaphore_wait(barrier, count)

    def inputs_to(nl, ny, slot, sender):
        to_head = 2 * ny + nl
        target = (dp, nl * NY + ny)
        rows = at(sender, TOK)
        pairs = (
            (k.at[:, at(to_head, HD)], ks.at[rows, :]),
            (q.at[:, at(to_head, 2 * HD)], qs.at[rows, :]),
            (v.at[:, at(to_head, HD)], vs.at[rows, :]),
            (do.at[:, at(to_head, 2 * HD)], dos.at[rows, :]),
            (seg, segs.at[sender]),
        )
        return [
            remote(src, dst, asend.at[index, slot], arecv.at[index, sender], target)
            for index, (src, dst) in enumerate(pairs)
        ]

    input_copies = []
    for slot, (dl, dy) in enumerate(PEERS):
        input_copies += inputs_to((zl + dl) % 2, (y + dy) % NY, slot, ctx)
    for copy in input_copies:
        copy.start()

    local_in[0].wait()
    for tile in range(feats // 128):
        turned = jnp.transpose(hv[:, tile * 128 : (tile + 1) * 128])
        row = tile * 128
        while row < (tile + 1) * 128:
            block = row // xrows
            stop = min((block + 1) * xrows, (tile + 1) * 128)
            start = (block // 2) * xrows + row - block * xrows
            hs[block % 2, start : start + stop - row, :] = turned[
                row - tile * 128 : stop - tile * 128, :
            ]
            row = stop

    h_across = remote(
        hs.at[other], hall.at[:, own], hsend.at[0], hrecv.at[ctx], (dp, partner)
    )
    h_across.start()
    h_own = pltpu.make_async_copy(hs.at[zl], hall.at[:, own], lsem.at[6])
    h_own.start()
    h_copies = [
        remote(
            hs.at[zl], hall.at[:, own], hsend.at[dy], hrecv.at[ctx],
            (dp, zl * NY + (y + dy) % NY),
        )
        for dy in (2, 1, 3)
    ]
    theirs = at(partner, TOK)
    h_passed = [
        remote(
            hall.at[:, theirs], hall.at[:, theirs], hsend.at[NY - 1 + dy], hrecv.at[partner],
            (dp, zl * NY + (y + dy) % NY),
        )
        for dy in (2, 1, 3)
    ]
    h_from_partner = remote(
        hs.at[other], hall.at[:, theirs], hsend.at[0], hrecv.at[partner], (dp, partner)
    )

    for copy in local_in[1:]:
        copy.wait()

    def out_copy(index, src, dst, block):
        return (
            remote(src, dst, osend.at[index, block], orecv.at[index, ctx], (dp, block)),
            pltpu.make_async_copy(src, dst, osend.at[index, block]),
        )

    def out_sends(block):
        rows = pl.ds(block * TOK, TOK)
        return (
            out_copy(0, dqs.at[rows, :], dq_out.at[:, at(head, 2 * HD)], block),
            out_copy(1, g4.at[zl, rows, :], dk_out.at[:, at(head, HD)], block),
            out_copy(2, g4.at[2 + zl, rows, :], dv_out.at[:, at(head, HD)], block),
        )

    def start_out(index, block):
        far, near = out_sends(block)[index]

        @pl.when(ctx != block)
        def _():
            far.start()

        @pl.when(ctx == block)
        def _():
            near.start()

    def trade(block, mine):
        rows = pl.ds(block * TOK, TOK)
        which = zl if mine else other
        return [
            remote(
                g4.at[2 * kind + which, rows, :], g4.at[2 * kind + which, rows, :],
                gsend.at[kind, block], grecv.at[kind, block], (dp, partner),
            )
            for kind in range(2)
        ]

    def finish_keys(block):
        rows = slice(block * TOK, (block + 1) * TOK)
        g4[zl, rows, :] = (dka[rows, :] * SCALE).astype(BF16)
        g4[2 + zl, rows, :] = dva[rows, :].astype(BF16)
        for copy in trade(block, True):
            copy.start()
        start_out(1, block)
        start_out(2, block)

    key_iota = lax.broadcasted_iota(jnp.int32, (TOK, 2 * TOK), 0)
    query_iota = lax.broadcasted_iota(jnp.int32, (TOK, 2 * TOK), 1)
    causal = key_iota <= query_iota % TOK

    for block in range(CTX):
        @pl.when(ctx != block)
        def _():
            for copy in inputs_to(zl, y, 0, block):
                copy.wait_recv()

        if block == 1:
            for copy in h_copies:
                copy.start()
        if block == 5:
            h_from_partner.wait_recv()
            for copy in h_passed:
                copy.start()

        first = max(0, block - SPAN)
        rows = slice(block * TOK, (block + 1) * TOK)
        band = slice(first * TOK, (block + 1) * TOK)
        deep = (block - first) * TOK
        seg_row = segs[block].astype(F32)
        segc[rows, :] = jnp.transpose(jnp.broadcast_to(seg_row, (TOK, TOK)))
        seg_row = jnp.concatenate([seg_row, seg_row], axis=1)
        seg_col = segc[band, :]
        seg_col = jnp.concatenate([seg_col, seg_col], axis=1)
        q2 = jnp.concatenate([qs[rows, :HD], qs[rows, HD:]], axis=0)
        do2 = jnp.concatenate([dos[rows, :HD], dos[rows, HD:]], axis=0)
        kw = ks[band, :]
        same = seg_col == seg_row
        scores = dot(kw, q2, NT)
        last = jnp.where(same[deep:] & causal, scores[deep:], FLOOR)
        if deep:
            scores = jnp.concatenate([jnp.where(same[:deep], scores[:deep], FLOOR), last], axis=0)
        else:
            scores = last
        peak = jnp.max(scores, axis=0, keepdims=True)
        weights = jnp.exp2((scores - peak) * EXP2_SCALE)
        probs = weights * (1.0 / jnp.sum(weights, axis=0, keepdims=True))
        probs_b = probs.astype(BF16)
        dprobs = dot(vs[band, :], do2, NT)
        delta = jnp.sum(probs_b.astype(F32) * dprobs, axis=0, keepdims=True)
        dscores = (probs * (dprobs - delta)).astype(BF16)
        dq2 = (dot(dscores, kw, TN) * SCALE).astype(BF16)
        dqs[rows, :HD] = dq2[:TOK]
        dqs[rows, HD:] = dq2[TOK:]
        start_out(0, block)
        dk_add = dot(dscores, q2)
        dv_add = dot(probs_b, do2)
        dka[rows, :] = dk_add[deep:]
        dva[rows, :] = dv_add[deep:]
        if deep:
            before = slice(first * TOK, block * TOK)
            dka[before, :] += dk_add[:deep]
            dva[before, :] += dv_add[:deep]
        if block >= SPAN:
            finish_keys(block - SPAN)
    for block in range(CTX - SPAN, CTX):
        finish_keys(block)

    h_own.wait()
    for dl in range(2):
        for dy in range(1, NY):
            sender = ((zl + dl) % 2) * NY + (y + dy) % NY
            remote(
                hs.at[zl], hall.at[:, at(sender, TOK)], hsend.at[0], hrecv.at[sender], (dp, partner)
            ).wait_recv()
    for block in range(CTX):
        for copy in trade(block, False):
            copy.wait_recv()

    def columns(kind):
        return jnp.concatenate([g4[2 * kind], g4[2 * kind + 1]], axis=1)

    far_core = (core + 1) % NC

    def core_copy(block):
        return remote(
            csend.at[block], crecv.at[block], csem.at[block], crsem.at[block],
            place(x, zh, far_core, zl, y),
        )

    for step in range(1, NX + 1):
        block = (x + step) % NX
        csend[block] = dot(hall[at(block, xrows), :], columns(far_core)).astype(BF16)
        core_copy(block).start()

    def x_copy(step, block):
        return remote(
            xsend.at[step], xrecv.at[step], xsem.at[step], xrsem.at[step],
            place(block, zh, core, zl, y),
        )

    for step in range(1, NX + 1):
        block = (x + step) % NX
        wown[...] = dot(hall[at(block, xrows), :], columns(core))
        core_copy(block).wait_recv()
        if step < NX:
            xsend[step - 1] = (wown[...] + crecv[block].astype(F32)).astype(BF16)
            x_copy(step - 1, block).start()
        else:
            tsum[:xrows, :] = wown[...] + crecv[block].astype(F32)
    for step in range(NX - 1):
        x_copy(step, x).wait_recv()
    tsum[:xrows, :] += (
        xrecv[0].astype(F32) + xrecv[1].astype(F32) + xrecv[2].astype(F32)
    )
    tsum[xrows:, :] = jnp.zeros((tsum.shape[0] - xrows, tsum.shape[1]), F32)

    def z_copies(piece):
        nz = 2 * zl + piece // 2
        nc = piece % 2
        mine = (nz == zh) & (nc == core) & (core == zl)
        return (
            mine,
            remote(
                zsend.at[piece], zrecv.at[zh], zsem.at[piece], zrsem.at[zh],
                place(x, nz, nc, core, y),
            ),
            pltpu.make_async_copy(zsend.at[piece], zrecv.at[zh], zsem.at[piece]),
        )

    for piece in range(4):
        zsend[piece] = tsum[piece * frows : piece * frows + zrows, :].astype(BF16)
        mine, far, near = z_copies(piece)

        @pl.when(mine)
        def _():
            near.start()

        @pl.when(jnp.logical_not(mine))
        def _():
            far.start()

    for piece in range(4):
        mine, far, near = z_copies(piece)

        @pl.when(mine)
        def _():
            near.wait()

        @pl.when(jnp.logical_not(mine))
        def _():
            far.wait_send()

    for sender in range(NZ):
        mine = (sender == zh) & (core == zl) & (zh // 2 == zl)

        @pl.when(jnp.logical_not(mine))
        def _():
            remote(
                zsend.at[0], zrecv.at[sender], zsem.at[0], zrsem.at[sender],
                place(x, zh, core, zl, y),
            ).wait_recv()

    w_out[...] = (
        (zrecv[0, :frows, :].astype(F32) + zrecv[1, :frows, :].astype(F32))
        + (zrecv[2, :frows, :].astype(F32) + zrecv[3, :frows, :].astype(F32))
    )

    for block in range(CTX):
        for index in range(3):
            far, near = out_sends(block)[index]

            @pl.when(ctx != block)
            def _():
                far.wait_send()

            @pl.when(ctx == block)
            def _():
                near.wait()

        for copy in trade(block, True):
            copy.wait_send()
    for block in range(CTX):
        from_head = 2 * (block % NY) + block // NY
        rows = pl.ds(0, TOK)

        @pl.when(ctx != block)
        def _():
            for index, (src, dst) in enumerate((
                (dqs.at[rows, :], dq_out.at[:, at(from_head, 2 * HD)]),
                (g4.at[0, rows, :], dk_out.at[:, at(from_head, HD)]),
                (g4.at[0, rows, :], dv_out.at[:, at(from_head, HD)]),
            )):
                remote(src, dst, osend.at[index, 0], orecv.at[index, block], (dp, partner)).wait_recv()

    for copy in input_copies + [h_across] + h_copies + h_passed:
        copy.wait_send()
    for step in range(1, NX + 1):
        core_copy((x + step) % NX).wait_send()
    for step in range(NX - 1):
        x_copy(step, x).wait_send()


def local(hidden_in, queries, key_states, value_states, out_grad, segment_ids):
    feats = hidden_in.shape[2]
    width = queries.shape[2]
    key_width = key_states.shape[2]
    half = feats // 2
    xrows = half // NX
    frows = feats // (NX * NZ * NC)
    zrows = -(-frows // 16) * 16
    seq = CTX * TOK
    any_spec = pl.BlockSpec(memory_space=pl.ANY)
    dma = pltpu.SemaphoreType.DMA
    scratch = [
        pltpu.VMEM((TOK, feats), BF16),
        pltpu.VMEM((seq, 2 * HD), BF16),
        pltpu.VMEM((seq, 2 * HD), BF16),
        pltpu.VMEM((seq, HD), BF16),
        pltpu.VMEM((seq, HD), BF16),
        pltpu.VMEM((CTX, 1, TOK), jnp.int32),
        pltpu.VMEM((seq, TOK), F32),
        pltpu.VMEM((seq, 2 * HD), BF16),
        pltpu.VMEM((4, seq, HD), BF16),
        pltpu.VMEM((seq, HD), F32),
        pltpu.VMEM((seq, HD), F32),
        pltpu.VMEM((2, half, TOK), BF16),
        pltpu.VMEM((half, seq), BF16),
        pltpu.VMEM((xrows, 2 * HD), F32),
        pltpu.VMEM((NX, xrows, 2 * HD), BF16),
        pltpu.VMEM((NX, xrows, 2 * HD), BF16),
        pltpu.VMEM((NX - 1, xrows, 2 * HD), BF16),
        pltpu.VMEM((NX - 1, xrows, 2 * HD), BF16),
        pltpu.VMEM((xrows + 16, 2 * HD), F32),
        pltpu.VMEM((4, zrows, 2 * HD), BF16),
        pltpu.VMEM((NZ, zrows, 2 * HD), BF16),
        dma((7,)),
        dma((5, 7)), dma((5, CTX)),
        dma((3, CTX)), dma((3, CTX)),
        dma((2, CTX)), dma((2, CTX)),
        dma((7,)), dma((CTX,)),
        dma((NX,)), dma((NX,)),
        dma((NX - 1,)), dma((NX - 1,)),
        dma((4,)), dma((NZ,)),
    ]
    dq, dk, dv, dw = pl.pallas_call(
        kernel,
        out_shape=(
            jax.ShapeDtypeStruct((TOK, width), BF16),
            jax.ShapeDtypeStruct((TOK, key_width), BF16),
            jax.ShapeDtypeStruct((TOK, key_width), BF16),
            jax.ShapeDtypeStruct((frows, 2 * HD), F32),
        ),
        in_specs=[any_spec] * 6,
        out_specs=(any_spec, any_spec, any_spec, pl.BlockSpec(memory_space=pltpu.VMEM)),
        scratch_shapes=scratch,
        compiler_params=pltpu.CompilerParams(
            collective_id=0, has_side_effects=True, vmem_limit_bytes=48 << 20
        ),
    )(hidden_in[0], queries[0], key_states[0], value_states[0], out_grad[0], segment_ids)
    return dq[None], dk[None], dv[None], dw


def solution(mesh):
    row = P("dp", "ctx", None)
    return jax.shard_map(
        local,
        mesh=mesh,
        in_specs=(row, row, row, row, row, P("dp", "ctx")),
        out_specs=(row, row, row, P("dp", "ctx")),
        check_vma=False,
    )
```

```python
import functools

import jax
import jax.numpy as jnp
from jax import lax
from jax.experimental import pallas as pl
from jax.experimental.pallas import tpu as pltpu
from jax.sharding import PartitionSpec as P

HD = 128
TOK = 128
CTX = 8
NY = 4
NX = 4
NZ = 4
NC = 2
SPAN = 4
FLOOR = -1e30
SCALE = HD ** (-0.5)
EXP2_SCALE = SCALE * 1.4426950408889634
MESH = pl.DeviceIdType.MESH
F32 = jnp.float32
BF16 = jnp.bfloat16
PEERS = ((1, 2), (0, 2), (1, 1), (1, 3), (0, 1), (0, 3), (1, 0))
NT = (((1,), (1,)), ((), ()))
TN = (((0,), (0,)), ((), ()))


def dot(lhs, rhs, dims=(((1,), (0,)), ((), ()))):
    return lax.dot_general(lhs, rhs, dims, preferred_element_type=F32)


def kernel(
    h, q, k, v, do, seg, dq_out, dk_out, dv_out, w_out,
    hv, qs, dos, ks, vs, segs, segc, dqs, g4, dka, dva, hs, hall,
    wown, csend, crecv, xsend, xrecv, tsum, zsend, zrecv,
    lsem, asend, arecv, osend, orecv, gsend, grecv,
    hasend, harecv, hysend, hyrecv, hpsend, hprecv,
    csem, crsem, xsem, xrsem, zsem, zrsem,
):
    feats = h.shape[1]
    half = feats // 2
    xrows = half // NX
    frows = w_out.shape[0]
    zrows = zsend.shape[1]
    split = (xrows // 2 + 15) // 16 * 16
    dp = lax.axis_index("dp")
    ctx = lax.axis_index("ctx")
    x = dp // (NZ * NC)
    zh = (dp // NC) % NZ
    core = dp % NC
    zl = ctx // NY
    y = ctx % NY
    other = (zl + 1) % 2
    head = 2 * y + zl
    partner = other * NY + y

    def at(place, width):
        return pl.ds(pl.multiple_of(place * width, width), width)

    def place(nx, nz, nc, nl, ny):
        return ((nx * NZ + nz) * NC + nc, nl * NY + ny)

    def remote(src, dst, ssem, rsem, device):
        return pltpu.make_async_remote_copy(
            src_ref=src, dst_ref=dst, send_sem=ssem, recv_sem=rsem,
            device_id=device, device_id_type=MESH,
        )

    barrier = pltpu.get_barrier_semaphore()
    count = 0
    for dz in range(NZ):
        for dc in range(NC):
            for dl in range(2):
                if dz + dc + dl:
                    pl.semaphore_signal(
                        barrier, inc=1, device_id_type=MESH,
                        device_id=place(x, (zh + dz) % NZ, (core + dc) % NC, (zl + dl) % 2, y),
                    )
                    count += 1
    for dl in range(2):
        for dy in range(1, NY):
            pl.semaphore_signal(
                barrier, inc=1, device_id_type=MESH,
                device_id=place(x, zh, core, (zl + dl) % 2, (y + dy) % NY),
            )
            count += 1
    for dx in range(1, NX):
        pl.semaphore_signal(
            barrier, inc=1, device_id_type=MESH,
            device_id=place((x + dx) % NX, zh, core, zl, y),
        )
        count += 1

    own = at(ctx, TOK)
    local_in = [
        pltpu.make_async_copy(h, hv, lsem.at[0]),
        pltpu.make_async_copy(q.at[:, at(head, 2 * HD)], qs.at[own, :], lsem.at[1]),
        pltpu.make_async_copy(do.at[:, at(head, 2 * HD)], dos.at[own, :], lsem.at[2]),
        pltpu.make_async_copy(k.at[:, at(head, HD)], ks.at[own, :], lsem.at[3]),
        pltpu.make_async_copy(v.at[:, at(head, HD)], vs.at[own, :], lsem.at[4]),
        pltpu.make_async_copy(seg, segs.at[ctx], lsem.at[5]),
    ]
    for copy in local_in:
        copy.start()
    pl.semaphore_wait(barrier, count)

    def inputs_to(nl, ny, slot, sender):
        to_head = 2 * ny + nl
        target = (dp, nl * NY + ny)
        rows = at(sender, TOK)
        pairs = (
            (k.at[:, at(to_head, HD)], ks.at[rows, :]),
            (q.at[:, at(to_head, 2 * HD)], qs.at[rows, :]),
            (v.at[:, at(to_head, HD)], vs.at[rows, :]),
            (do.at[:, at(to_head, 2 * HD)], dos.at[rows, :]),
            (seg, segs.at[sender]),
        )
        return [
            remote(src, dst, asend.at[index, slot], arecv.at[index, sender], target)
            for index, (src, dst) in enumerate(pairs)
        ]

    input_copies = []
    for slot, (dl, dy) in enumerate(PEERS):
        input_copies += inputs_to((zl + dl) % 2, (y + dy) % NY, slot, ctx)
    for copy in input_copies:
        copy.start()

    local_in[0].wait()
    for tile in range(feats // 128):
        turned = jnp.transpose(hv[:, tile * 128 : (tile + 1) * 128])
        row = tile * 128
        while row < (tile + 1) * 128:
            block = row // xrows
            stop = min((block + 1) * xrows, (tile + 1) * 128)
            start = (block // 2) * xrows + row - block * xrows
            hs[block % 2, start : start + stop - row, :] = turned[
                row - tile * 128 : stop - tile * 128, :
            ]
            row = stop

    h_own = pltpu.make_async_copy(hs.at[zl], hall.at[:, own], lsem.at[6])
    h_own.start()

    def chunk(step):
        return (x + step + 1) % NX * xrows

    def h_rows(step, part=None):
        start, size = (0, xrows) if part is None else ((0, split), (split, xrows - split))[part]
        return pl.ds(pl.multiple_of(chunk(step) + start, 16), size)

    def h_across(step, block):
        return remote(
            hs.at[other, h_rows(step), :], hall.at[h_rows(step), at(block, TOK)],
            hasend.at[step], harecv.at[step], (dp, partner),
        )

    def h_block(kind, ny):
        return (zl + kind) % 2 * NY + (ny + NY) % NY

    def h_step(step, kind, way, ny):
        cols = at(h_block(kind, ny), TOK)
        src = hall.at[h_rows(step), cols] if kind else hs.at[zl, h_rows(step), :]
        return remote(
            src, hall.at[h_rows(step), cols], hysend.at[step, kind, way],
            hyrecv.at[step, kind, way], (dp, zl * NY + (y + 1 + 2 * way) % NY),
        )

    def h_pass(step, kind, way, ny):
        place_of = hall.at[h_rows(step, way), at(h_block(kind, ny), TOK)]
        return remote(
            place_of, place_of, hpsend.at[step, kind, way],
            hprecv.at[step, kind, way], (dp, zl * NY + (y + 1 + 2 * way) % NY),
        )

    def h_start(step, kind):
        for way in range(2):
            h_step(step, kind, way, y).start()

    def h_forward(step, kind):
        for way in range(2):
            came_from = y - 1 + 2 * way
            h_step(step, kind, way, came_from).wait_recv()
            h_pass(step, kind, way, came_from).start()

    def h_arrive(step):
        for kind in range(2):
            for way in range(2):
                h_pass(step, kind, way, y + 2).wait_recv()

    def h_partner(step):
        h_across(step, partner).wait_recv()
        h_start(step, 1)

    h_across(0, ctx).start()
    h_across(1, ctx).start()
    h_across(2, ctx).start()
    h_across(3, ctx).start()
    h_start(0, 0)
    h_start(1, 0)
    h_start(2, 0)
    h_start(3, 0)

    for copy in local_in[1:]:
        copy.wait()

    def out_refs(index, block):
        rows = pl.ds(block * TOK, TOK)
        return (
            (dqs.at[rows, :], dq_out.at[:, at(head, 2 * HD)]),
            (g4.at[zl, rows, :], dk_out.at[:, at(head, HD)]),
            (g4.at[2 + zl, rows, :], dv_out.at[:, at(head, HD)]),
        )[index]

    def out_far(index, block):
        return remote(
            *out_refs(index, block), osend.at[index, block], orecv.at[index, ctx], (dp, block)
        )

    def out_near(index, block):
        return pltpu.make_async_copy(*out_refs(index, block), osend.at[index, block])

    def start_out(index, block):
        @pl.when(ctx != block)
        def _():
            out_far(index, block).start()

        @pl.when(ctx == block)
        def _():
            out_near(index, block).start()

    def trade(block, mine):
        rows = pl.ds(block * TOK, TOK)
        which = zl if mine else other
        return [
            remote(
                g4.at[2 * kind + which, rows, :], g4.at[2 * kind + which, rows, :],
                gsend.at[kind, block], grecv.at[kind, block], (dp, partner),
            )
            for kind in range(2)
        ]

    def finish_keys(block):
        rows = slice(block * TOK, (block + 1) * TOK)
        g4[zl, rows, :] = (dka[rows, :] * SCALE).astype(BF16)
        g4[2 + zl, rows, :] = dva[rows, :].astype(BF16)
        for copy in trade(block, True):
            copy.start()

    key_iota = lax.broadcasted_iota(jnp.int32, (TOK, 2 * TOK), 0)
    query_iota = lax.broadcasted_iota(jnp.int32, (TOK, 2 * TOK), 1)
    causal = key_iota <= query_iota % TOK

    for block in range(CTX):
        @pl.when(ctx != block)
        def _():
            for copy in inputs_to(zl, y, 0, block):
                copy.wait_recv()

        if block == 5:
            h_forward(0, 0)
            h_forward(1, 0)
        if block == 6:
            h_partner(0)
            h_partner(1)
        if block == 7:
            h_partner(2)
            h_partner(3)

        first = max(0, block - SPAN)
        rows = slice(block * TOK, (block + 1) * TOK)
        band = slice(first * TOK, (block + 1) * TOK)
        deep = (block - first) * TOK
        seg_row = segs[block].astype(F32)
        segc[rows, :] = jnp.transpose(jnp.broadcast_to(seg_row, (TOK, TOK)))
        seg_row = jnp.concatenate([seg_row, seg_row], axis=1)
        seg_col = segc[band, :]
        seg_col = jnp.concatenate([seg_col, seg_col], axis=1)
        q2 = jnp.concatenate([qs[rows, :HD], qs[rows, HD:]], axis=0)
        do2 = jnp.concatenate([dos[rows, :HD], dos[rows, HD:]], axis=0)
        kw = ks[band, :]
        same = seg_col == seg_row
        scores = dot(kw, q2, NT)
        last = jnp.where(same[deep:] & causal, scores[deep:], FLOOR)
        if deep:
            scores = jnp.concatenate([jnp.where(same[:deep], scores[:deep], FLOOR), last], axis=0)
        else:
            scores = last
        peak = jnp.max(scores, axis=0, keepdims=True)
        weights = jnp.exp2((scores - peak) * EXP2_SCALE)
        probs = weights * (1.0 / jnp.sum(weights, axis=0, keepdims=True))
        probs_b = probs.astype(BF16)
        dprobs = dot(vs[band, :], do2, NT)
        delta = jnp.sum(probs_b.astype(F32) * dprobs, axis=0, keepdims=True)
        dscores = (probs * (dprobs - delta)).astype(BF16)
        dq2 = (dot(dscores, kw, TN) * SCALE).astype(BF16)
        dqs[rows, :HD] = dq2[:TOK]
        dqs[rows, HD:] = dq2[TOK:]
        dk_add = dot(dscores, q2)
        dv_add = dot(probs_b, do2)
        dka[rows, :] = dk_add[deep:]
        dva[rows, :] = dv_add[deep:]
        if deep:
            before = slice(first * TOK, block * TOK)
            dka[before, :] += dk_add[:deep]
            dva[before, :] += dv_add[:deep]
        if block >= SPAN:
            finish_keys(block - SPAN)
    for block in range(CTX - SPAN, CTX):
        finish_keys(block)

    def columns(kind):
        return jnp.concatenate([g4[2 * kind], g4[2 * kind + 1]], axis=1)

    far_core = (core + 1) % NC

    def core_copy(block):
        return remote(
            csend.at[block], crecv.at[block], csem.at[block], crsem.at[block],
            place(x, zh, far_core, zl, y),
        )

    def x_copy(step, block):
        return remote(
            xsend.at[step], xrecv.at[step], xsem.at[step], xrsem.at[step],
            place(block, zh, core, zl, y),
        )

    def weights_far(step):
        block = (x + step + 1) % NX
        h_arrive(step)
        if step == 0:
            h_own.wait()
            for block_in in range(CTX):
                for copy in trade(block_in, False):
                    copy.wait_recv()
        csend[block] = dot(hall[at(block, xrows), :], columns(far_core)).astype(BF16)
        core_copy(block).start()

    def weights_own(step):
        block = (x + step + 1) % NX
        wown[...] = dot(hall[at(block, xrows), :], columns(core))
        core_copy(block).wait_recv()
        if step < NX - 1:
            xsend[step] = (wown[...] + crecv[block].astype(F32)).astype(BF16)
            x_copy(step, block).start()
        else:
            tsum[:xrows, :] = wown[...] + crecv[block].astype(F32)

    def give_back():
        for block in range(CTX):
            for index in range(3):
                start_out(index, block)

    h_forward(2, 0)
    h_forward(3, 0)
    h_forward(0, 1)
    h_forward(1, 1)
    h_forward(2, 1)
    weights_far(0)
    h_forward(3, 1)
    weights_far(1)
    weights_own(0)
    give_back()
    weights_far(2)
    weights_own(1)
    weights_far(3)
    weights_own(2)
    weights_own(3)

    for step in range(NX - 1):
        x_copy(step, x).wait_recv()
    tsum[:xrows, :] += (
        xrecv[0].astype(F32) + xrecv[1].astype(F32) + xrecv[2].astype(F32)
    )
    tsum[xrows:, :] = jnp.zeros((tsum.shape[0] - xrows, tsum.shape[1]), F32)

    def z_mine(piece):
        return (2 * zl + piece // 2 == zh) & (piece % 2 == core) & (core == zl)

    def z_far(piece):
        return remote(
            zsend.at[piece], zrecv.at[zh], zsem.at[piece], zrsem.at[zh],
            place(x, 2 * zl + piece // 2, piece % 2, core, y),
        )

    def z_near(piece):
        return pltpu.make_async_copy(zsend.at[piece], zrecv.at[zh], zsem.at[piece])

    for piece in range(4):
        zsend[piece] = tsum[piece * frows : piece * frows + zrows, :].astype(BF16)

        @pl.when(z_mine(piece))
        def _():
            z_near(piece).start()

        @pl.when(jnp.logical_not(z_mine(piece)))
        def _():
            z_far(piece).start()

    for piece in range(4):
        @pl.when(z_mine(piece))
        def _():
            z_near(piece).wait()

        @pl.when(jnp.logical_not(z_mine(piece)))
        def _():
            z_far(piece).wait_send()

    for sender in range(NZ):
        mine = (sender == zh) & (core == zl) & (zh // 2 == zl)

        @pl.when(jnp.logical_not(mine))
        def _():
            remote(
                zsend.at[0], zrecv.at[sender], zsem.at[0], zrsem.at[sender],
                place(x, zh, core, zl, y),
            ).wait_recv()

    w_out[...] = (
        (zrecv[0, :frows, :].astype(F32) + zrecv[1, :frows, :].astype(F32))
        + (zrecv[2, :frows, :].astype(F32) + zrecv[3, :frows, :].astype(F32))
    )

    for block in range(CTX):
        for index in range(3):
            @pl.when(ctx != block)
            def _():
                out_far(index, block).wait_send()

            @pl.when(ctx == block)
            def _():
                out_near(index, block).wait()

        for copy in trade(block, True):
            copy.wait_send()
    for block in range(CTX):
        from_head = 2 * (block % NY) + block // NY
        rows = pl.ds(0, TOK)

        @pl.when(ctx != block)
        def _():
            for index, (src, dst) in enumerate((
                (dqs.at[rows, :], dq_out.at[:, at(from_head, 2 * HD)]),
                (g4.at[0, rows, :], dk_out.at[:, at(from_head, HD)]),
                (g4.at[0, rows, :], dv_out.at[:, at(from_head, HD)]),
            )):
                remote(src, dst, osend.at[index, 0], orecv.at[index, block], (dp, partner)).wait_recv()

    for copy in input_copies:
        copy.wait_send()
    for step in range(NX):
        h_across(step, ctx).wait_send()
        for kind in range(2):
            for way in range(2):
                h_step(step, kind, way, y).wait_send()
                h_pass(step, kind, way, y - 1 + 2 * way).wait_send()
    for step in range(1, NX + 1):
        core_copy((x + step) % NX).wait_send()
    for step in range(NX - 1):
        x_copy(step, x).wait_send()


def hand_over(*refs):
    sources, targets, stages = refs[:4], refs[4:8], refs[8:12]
    sems = refs[12]
    loads = [
        pltpu.make_async_copy(src, stage, sems.at[0, index])
        for index, (src, stage) in enumerate(zip(sources, stages))
    ]
    stores = [
        pltpu.make_async_copy(stage, dst, sems.at[1, index])
        for index, (stage, dst) in enumerate(zip(stages, targets))
    ]
    for copy in loads:
        copy.start()
    for load, store in zip(loads, stores):
        load.wait()
        store.start()
    for copy in stores:
        copy.wait()


def local(hidden_in, queries, key_states, value_states, out_grad, segment_ids):
    feats = hidden_in.shape[2]
    width = queries.shape[2]
    key_width = key_states.shape[2]
    half = feats // 2
    xrows = half // NX
    frows = feats // (NX * NZ * NC)
    zrows = -(-frows // 16) * 16
    seq = CTX * TOK
    any_spec = pl.BlockSpec(memory_space=pltpu.HBM)
    dma = pltpu.SemaphoreType.DMA
    scratch = [
        pltpu.VMEM((TOK, feats), BF16),
        pltpu.VMEM((seq, 2 * HD), BF16),
        pltpu.VMEM((seq, 2 * HD), BF16),
        pltpu.VMEM((seq, HD), BF16),
        pltpu.VMEM((seq, HD), BF16),
        pltpu.VMEM((CTX, 1, TOK), jnp.int32),
        pltpu.VMEM((seq, TOK), F32),
        pltpu.VMEM((seq, 2 * HD), BF16),
        pltpu.VMEM((4, seq, HD), BF16),
        pltpu.VMEM((seq, HD), F32),
        pltpu.VMEM((seq, HD), F32),
        pltpu.VMEM((2, half, TOK), BF16),
        pltpu.VMEM((half, seq), BF16),
        pltpu.VMEM((xrows, 2 * HD), F32),
        pltpu.VMEM((NX, xrows, 2 * HD), BF16),
        pltpu.VMEM((NX, xrows, 2 * HD), BF16),
        pltpu.VMEM((NX - 1, xrows, 2 * HD), BF16),
        pltpu.VMEM((NX - 1, xrows, 2 * HD), BF16),
        pltpu.VMEM((xrows + 16, 2 * HD), F32),
        pltpu.VMEM((4, zrows, 2 * HD), BF16),
        pltpu.VMEM((NZ, zrows, 2 * HD), BF16),
        dma((7,)),
        dma((5, 7)), dma((5, CTX)),
        dma((3, CTX)), dma((3, CTX)),
        dma((2, CTX)), dma((2, CTX)),
        dma((NX,)), dma((NX,)),
        dma((NX, 2, 2)), dma((NX, 2, 2)),
        dma((NX, 2, 2)), dma((NX, 2, 2)),
        dma((NX,)), dma((NX,)),
        dma((NX - 1,)), dma((NX - 1,)),
        dma((4,)), dma((NZ,)),
    ]
    outs = (
        jax.ShapeDtypeStruct((TOK, width), BF16),
        jax.ShapeDtypeStruct((TOK, key_width), BF16),
        jax.ShapeDtypeStruct((TOK, key_width), BF16),
        jax.ShapeDtypeStruct((frows, 2 * HD), F32),
    )
    parts = pl.pallas_call(
        kernel,
        out_shape=outs,
        in_specs=[any_spec] * 6,
        out_specs=(any_spec, any_spec, any_spec, pl.BlockSpec(memory_space=pltpu.VMEM)),
        scratch_shapes=scratch,
        compiler_params=pltpu.CompilerParams(
            collective_id=0, has_side_effects=True, vmem_limit_bytes=63 << 20
        ),
    )(hidden_in[0], queries[0], key_states[0], value_states[0], out_grad[0], segment_ids)
    dq, dk, dv, dw = pl.pallas_call(
        hand_over,
        out_shape=outs,
        in_specs=[any_spec] * 4,
        out_specs=(any_spec,) * 4,
        scratch_shapes=[pltpu.VMEM(out.shape, out.dtype) for out in outs] + [dma((2, 4))],
    )(*parts)
    return dq[None], dk[None], dv[None], dw


def solution(mesh):
    row = P("dp", "ctx", None)
    return jax.shard_map(
        local,
        mesh=mesh,
        in_specs=(row, row, row, row, row, P("dp", "ctx")),
        out_specs=(row, row, row, P("dp", "ctx")),
        check_vma=False,
    )
```

```python
import functools

import jax
import jax.numpy as jnp
from jax import lax
from jax.experimental import pallas as pl
from jax.experimental.pallas import tpu as pltpu
from jax.sharding import PartitionSpec as P

HD = 128
TOK = 128
CTX = 8
NY = 4
NX = 4
NZ = 4
NC = 2
SPAN = 4
FLOOR = -1e30
SCALE = HD ** (-0.5)
EXP2_SCALE = SCALE * 1.4426950408889634
MESH = pl.DeviceIdType.MESH
F32 = jnp.float32
BF16 = jnp.bfloat16
PEERS = ((1, 2), (0, 2), (1, 1), (1, 3), (0, 1), (0, 3), (1, 0))
ORDER = (1, 2, 3, 0)
NT = (((1,), (1,)), ((), ()))
TN = (((0,), (0,)), ((), ()))


def dot(lhs, rhs, dims=(((1,), (0,)), ((), ()))):
    return lax.dot_general(lhs, rhs, dims, preferred_element_type=F32)


def kernel(
    h, q, k, v, do, seg, dq_out, dk_out, dv_out, w_out,
    hv, qs, dos, ks, vs, segs, segc, dqs, g4, dka, dva, hs, hall,
    csend, crecv, xsend, xrecv, tsum, zsend, zrecv,
    lsem, asend, arecv, osend, orecv, gsend, grecv,
    hsend, harecv, hyrecv, hprecv,
    csem, crsem, xsem, xrsem, zsem, zrsem,
):
    feats = h.shape[1]
    half = feats // 2
    xrows = half // NX
    frows = w_out.shape[0]
    zrows = zsend.shape[1]
    split = (xrows // 2 + 15) // 16 * 16
    dp = lax.axis_index("dp")
    ctx = lax.axis_index("ctx")
    x = dp // (NZ * NC)
    zh = (dp // NC) % NZ
    core = dp % NC
    zl = ctx // NY
    y = ctx % NY
    other = (zl + 1) % 2
    head = 2 * y + zl
    partner = other * NY + y

    def at(place, width):
        return pl.ds(pl.multiple_of(place * width, width), width)

    def place(nx, nz, nc, nl, ny):
        return ((nx * NZ + nz) * NC + nc, nl * NY + ny)

    def remote(src, dst, ssem, rsem, device):
        return pltpu.make_async_remote_copy(
            src_ref=src, dst_ref=dst, send_sem=ssem, recv_sem=rsem,
            device_id=device, device_id_type=MESH,
        )

    def drain(sem, rows, cols):
        whole = hall.at[pl.ds(0, rows), pl.ds(0, cols)]
        pltpu.make_async_copy(whole, whole, sem).wait()

    barrier = pltpu.get_barrier_semaphore()
    count = 0
    for dz in range(NZ):
        for dc in range(NC):
            for dl in range(2):
                if dz + dc + dl:
                    pl.semaphore_signal(
                        barrier, inc=1, device_id_type=MESH,
                        device_id=place(x, (zh + dz) % NZ, (core + dc) % NC, (zl + dl) % 2, y),
                    )
                    count += 1
    for dl in range(2):
        for dy in range(1, NY):
            pl.semaphore_signal(
                barrier, inc=1, device_id_type=MESH,
                device_id=place(x, zh, core, (zl + dl) % 2, (y + dy) % NY),
            )
            count += 1
    for dx in range(1, NX):
        pl.semaphore_signal(
            barrier, inc=1, device_id_type=MESH,
            device_id=place((x + dx) % NX, zh, core, zl, y),
        )
        count += 1

    own = at(ctx, TOK)
    local_in = [
        pltpu.make_async_copy(h, hv, lsem.at[0]),
        pltpu.make_async_copy(q.at[:, at(head, 2 * HD)], qs.at[own, :], lsem.at[1]),
        pltpu.make_async_copy(do.at[:, at(head, 2 * HD)], dos.at[own, :], lsem.at[2]),
        pltpu.make_async_copy(k.at[:, at(head, HD)], ks.at[own, :], lsem.at[3]),
        pltpu.make_async_copy(v.at[:, at(head, HD)], vs.at[own, :], lsem.at[4]),
        pltpu.make_async_copy(seg, segs.at[ctx], lsem.at[5]),
    ]
    for copy in local_in:
        copy.start()
    pl.semaphore_wait(barrier, count)

    def inputs_to(nl, ny, sender, slot=0):
        to_head = 2 * ny + nl
        target = (dp, nl * NY + ny)
        rows = at(sender, TOK)
        pairs = (
            (k.at[:, at(to_head, HD)], ks.at[rows, :]),
            (q.at[:, at(to_head, 2 * HD)], qs.at[rows, :]),
            (v.at[:, at(to_head, HD)], vs.at[rows, :]),
            (do.at[:, at(to_head, 2 * HD)], dos.at[rows, :]),
            (seg, segs.at[sender]),
        )
        return [
            remote(src, dst, asend.at[index // 4 * (1 + slot)], arecv.at[index // 4, sender], target)
            for index, (src, dst) in enumerate(pairs)
        ]

    input_copies = []
    for slot, (dl, dy) in enumerate(PEERS):
        input_copies += inputs_to((zl + dl) % 2, (y + dy) % NY, ctx, slot)
    for copy in input_copies:
        copy.start()

    local_in[0].wait()
    for tile in range(feats // 128):
        turned = jnp.transpose(hv[:, tile * 128 : (tile + 1) * 128])
        row = tile * 128
        while row < (tile + 1) * 128:
            block = row // xrows
            stop = min((block + 1) * xrows, (tile + 1) * 128)
            start = (block // 2) * xrows + row - block * xrows
            hs[block % 2, start : start + stop - row, :] = turned[
                row - tile * 128 : stop - tile * 128, :
            ]
            row = stop

    h_own = pltpu.make_async_copy(hs.at[zl], hall.at[:, own], lsem.at[6])
    h_own.start()

    def x_of(step):
        return (x + ORDER[step]) % NX

    def chunk(step):
        return x_of(step) * xrows

    def h_rows(step, part=None):
        start, size = (0, xrows) if part is None else ((0, split), (split, xrows - split))[part]
        return pl.ds(pl.multiple_of(chunk(step) + start, 16), size)

    def h_across(step, block):
        return remote(
            hs.at[other, h_rows(step), :], hall.at[h_rows(step), at(block, TOK)],
            hsend.at[0], harecv.at[step], (dp, partner),
        )

    def h_block(kind, ny):
        return (zl + kind) % 2 * NY + (ny + NY) % NY

    def h_step(step, kind, way, ny):
        cols = at(h_block(kind, ny), TOK)
        src = hall.at[h_rows(step), cols] if kind else hs.at[zl, h_rows(step), :]
        return remote(
            src, hall.at[h_rows(step), cols], hsend.at[0],
            hyrecv.at[step, kind], (dp, zl * NY + (y + 1 + 2 * way) % NY),
        )

    def h_pass(step, kind, way, ny):
        place_of = hall.at[h_rows(step, way), at(h_block(kind, ny), TOK)]
        return remote(
            place_of, place_of, hsend.at[0],
            hprecv.at[step], (dp, zl * NY + (y + 1 + 2 * way) % NY),
        )

    def h_start(step, kind):
        for way in range(2):
            h_step(step, kind, way, y).start()

    def h_forward(step, kind):
        drain(hyrecv.at[step, kind], xrows, 2 * TOK)
        for way in range(2):
            h_pass(step, kind, way, y - 1 + 2 * way).start()

    def h_arrive(step):
        drain(hprecv.at[step], xrows, 2 * TOK)

    def h_partner(step):
        h_across(step, partner).wait_recv()
        h_start(step, 1)

    h_across(0, ctx).start()
    h_across(1, ctx).start()
    h_start(0, 0)
    h_start(1, 0)

    for copy in local_in[1:]:
        copy.wait()

    def out_refs(block):
        rows = at(block, TOK)
        return (
            (dqs.at[rows, :], dq_out.at[:, at(head, 2 * HD)]),
            (g4.at[zl, rows, :], dk_out.at[:, at(head, HD)]),
            (g4.at[2 + zl, rows, :], dv_out.at[:, at(head, HD)]),
        )

    def trade(block):
        rows = pl.ds(block * TOK, TOK)
        return [
            remote(
                g4.at[2 * kind + zl, rows, :], g4.at[2 * kind + zl, rows, :],
                gsend.at[0], grecv.at[0], (dp, partner),
            )
            for kind in range(2)
        ]

    def finish_keys(block):
        rows = slice(block * TOK, (block + 1) * TOK)
        g4[zl, rows, :] = (dka[rows, :] * SCALE).astype(BF16)
        g4[2 + zl, rows, :] = dva[rows, :].astype(BF16)
        for copy in trade(block):
            copy.start()

    key_iota = lax.broadcasted_iota(jnp.int32, (TOK, 2 * TOK), 0)
    query_iota = lax.broadcasted_iota(jnp.int32, (TOK, 2 * TOK), 1)
    causal = key_iota <= query_iota % TOK

    for block in range(CTX):
        @pl.when(ctx != block)
        def _():
            drain(arecv.at[0, block], 6 * TOK, TOK)
            inputs_to(zl, y, block)[4].wait_recv()

        if block == 1:
            h_across(2, ctx).start()
            h_across(3, ctx).start()
            h_start(2, 0)
            h_start(3, 0)
        if block == 5:
            h_forward(0, 0)
            h_forward(1, 0)
        if block == 6:
            h_partner(0)
            h_partner(1)
        if block == 7:
            h_partner(2)
            h_partner(3)

        first = max(0, block - SPAN)
        rows = slice(block * TOK, (block + 1) * TOK)
        band = slice(first * TOK, (block + 1) * TOK)
        deep = (block - first) * TOK
        seg_row = segs[block].astype(F32)
        segc[rows, :] = jnp.transpose(jnp.broadcast_to(seg_row, (TOK, TOK)))
        seg_row = jnp.concatenate([seg_row, seg_row], axis=1)
        seg_col = segc[band, :]
        seg_col = jnp.concatenate([seg_col, seg_col], axis=1)
        q2 = jnp.concatenate([qs[rows, :HD], qs[rows, HD:]], axis=0)
        do2 = jnp.concatenate([dos[rows, :HD], dos[rows, HD:]], axis=0)
        kw = ks[band, :]
        same = seg_col == seg_row
        scores = dot(kw, q2, NT)
        last = jnp.where(same[deep:] & causal, scores[deep:], FLOOR)
        if deep:
            scores = jnp.concatenate([jnp.where(same[:deep], scores[:deep], FLOOR), last], axis=0)
        else:
            scores = last
        peak = jnp.max(scores, axis=0, keepdims=True)
        weights = jnp.exp2((scores - peak) * EXP2_SCALE)
        probs = weights * (1.0 / jnp.sum(weights, axis=0, keepdims=True))
        probs_b = probs.astype(BF16)
        dprobs = dot(vs[band, :], do2, NT)
        delta = jnp.sum(probs_b.astype(F32) * dprobs, axis=0, keepdims=True)
        dscores = (probs * (dprobs - delta)).astype(BF16)
        dq2 = (dot(dscores, kw, TN) * SCALE).astype(BF16)
        dqs[rows, :HD] = dq2[:TOK]
        dqs[rows, HD:] = dq2[TOK:]
        dk_add = dot(dscores, q2)
        dv_add = dot(probs_b, do2)
        dka[rows, :] = dk_add[deep:]
        dva[rows, :] = dv_add[deep:]
        if deep:
            before = slice(first * TOK, block * TOK)
            dka[before, :] += dk_add[:deep]
            dva[before, :] += dv_add[:deep]
        if block >= SPAN:
            finish_keys(block - SPAN)
    for block in range(CTX - SPAN, CTX):
        finish_keys(block)

    for src, dst in out_refs(ctx):
        pltpu.make_async_copy(src, dst, lsem.at[0]).start()

    def columns(kind):
        return jnp.concatenate([g4[2 * kind], g4[2 * kind + 1]], axis=1)

    far_core = (core + 1) % NC

    def part_rows(part):
        return ((0, split), (split, xrows - split))[part]

    def core_copy(part, step):
        piece = (x_of(step), pl.ds(*part_rows(part)))
        return remote(
            csend.at[piece], crecv.at[piece], csem.at[0], crsem.at[step, part],
            place(x, zh, far_core, zl, y),
        )

    def x_copy(part, step, nx):
        piece = (step, pl.ds(*part_rows(part)))
        return remote(
            xsend.at[piece], xrecv.at[piece], xsem.at[0], xrsem.at[part],
            place(nx, zh, core, zl, y),
        )

    def weights_far(part, step):
        if part == 0:
            h_arrive(step)
        if part == 0 and step == 0:
            h_own.wait()
            drain(grecv.at[0], CTX * TOK, 2 * TOK)
        csend[x_of(step), pl.ds(*part_rows(part)), :] = dot(
            hall[h_rows(step, part), :], columns(far_core)
        ).astype(BF16)
        core_copy(part, step).start()

    def weights_own(part, step):
        rows = pl.ds(*part_rows(part))
        mine = dot(hall[h_rows(step, part), :], columns(core))
        core_copy(part, step).wait_recv()
        total = mine + crecv[x_of(step), rows, :].astype(F32)
        if step < NX - 1:
            xsend[step, rows, :] = total.astype(BF16)
            x_copy(part, step, x_of(step)).start()
        else:
            tsum[rows, :] = total

    def x_finish(part):
        rows = pl.ds(*part_rows(part))
        drain(xrsem.at[part], (NX - 1) * part_rows(part)[1], 2 * HD)
        tsum[rows, :] += (
            xrecv[0, rows, :].astype(F32) + xrecv[1, rows, :].astype(F32)
            + xrecv[2, rows, :].astype(F32)
        )
        for piece in (2 * part, 2 * part + 1):
            zsend[piece] = tsum[piece * frows : piece * frows + zrows, :].astype(BF16)

            @pl.when(z_mine(piece))
            def _():
                z_near(piece).start()

            @pl.when(jnp.logical_not(z_mine(piece)))
            def _():
                z_far(piece).start()

    def z_mine(piece):
        return (2 * zl + piece // 2 == zh) & (piece % 2 == core) & (core == zl)

    def z_far(piece):
        return remote(
            zsend.at[piece], zrecv.at[zh], zsem.at[piece], zrsem.at[zh],
            place(x, 2 * zl + piece // 2, piece % 2, core, y),
        )

    def z_near(piece):
        return pltpu.make_async_copy(zsend.at[piece], zrecv.at[zh], zsem.at[piece])

    def give_back(peers):
        for dl, dy in peers:
            block = (zl + dl) % 2 * NY + (y + dy) % NY
            for src, dst in out_refs(block):
                remote(src, dst, osend.at[0], orecv.at[0], (dp, block)).start()

    tsum[xrows:, :] = jnp.zeros((tsum.shape[0] - xrows, tsum.shape[1]), F32)
    h_forward(2, 0)
    h_forward(3, 0)
    h_forward(0, 1)
    h_forward(1, 1)
    h_forward(2, 1)
    weights_far(0, 0)
    h_forward(3, 1)
    weights_far(0, 1)
    weights_own(0, 0)
    give_back(PEERS)
    weights_far(0, 2)
    weights_own(0, 1)
    weights_far(0, 3)
    weights_own(0, 2)
    weights_own(0, 3)
    weights_far(1, 0)
    weights_far(1, 1)
    weights_own(1, 0)
    weights_far(1, 2)
    weights_own(1, 1)
    weights_far(1, 3)
    weights_own(1, 2)
    weights_own(1, 3)

    x_finish(0)
    x_finish(1)

    drain(asend.at[0], half, 4 * TOK)
    for copy in input_copies[4::5]:
        copy.wait_send()
    drain(hsend.at[0], half, 7 * TOK)
    drain(gsend.at[0], CTX * TOK, 2 * TOK)
    drain(csem.at[0], half, 2 * HD)
    drain(xsem.at[0], (NX - 1) * xrows, 2 * HD)
    drain(lsem.at[0], 4 * TOK, TOK)
    drain(osend.at[0], (CTX - 1) * TOK, 4 * TOK)
    drain(orecv.at[0], (CTX - 1) * TOK, 4 * TOK)

    for piece in range(4):
        @pl.when(z_mine(piece))
        def _():
            z_near(piece).wait()

        @pl.when(jnp.logical_not(z_mine(piece)))
        def _():
            z_far(piece).wait_send()

    for sender in range(NZ):
        mine = (sender == zh) & (core == zl) & (zh // 2 == zl)

        @pl.when(jnp.logical_not(mine))
        def _():
            remote(
                zsend.at[0], zrecv.at[sender], zsem.at[0], zrsem.at[sender],
                place(x, zh, core, zl, y),
            ).wait_recv()

    w_out[...] = (
        (zrecv[0, :frows, :].astype(F32) + zrecv[1, :frows, :].astype(F32))
        + (zrecv[2, :frows, :].astype(F32) + zrecv[3, :frows, :].astype(F32))
    )


def hand_over(*refs):
    sources, targets, stages = refs[:4], refs[4:8], refs[8:12]
    sems = refs[12]
    loads = [
        pltpu.make_async_copy(src, stage, sems.at[0, index])
        for index, (src, stage) in enumerate(zip(sources, stages))
    ]
    stores = [
        pltpu.make_async_copy(stage, dst, sems.at[1, index])
        for index, (stage, dst) in enumerate(zip(stages, targets))
    ]
    for copy in loads:
        copy.start()
    for load, store in zip(loads, stores):
        load.wait()
        store.start()
    for copy in stores:
        copy.wait()


def local(hidden_in, queries, key_states, value_states, out_grad, segment_ids):
    feats = hidden_in.shape[2]
    width = queries.shape[2]
    key_width = key_states.shape[2]
    half = feats // 2
    xrows = half // NX
    frows = feats // (NX * NZ * NC)
    zrows = -(-frows // 16) * 16
    seq = CTX * TOK
    any_spec = pl.BlockSpec(memory_space=pltpu.HBM)
    dma = pltpu.SemaphoreType.DMA
    scratch = [
        pltpu.VMEM((TOK, feats), BF16),
        pltpu.VMEM((seq, 2 * HD), BF16),
        pltpu.VMEM((seq, 2 * HD), BF16),
        pltpu.VMEM((seq, HD), BF16),
        pltpu.VMEM((seq, HD), BF16),
        pltpu.VMEM((CTX, 1, TOK), jnp.int32),
        pltpu.VMEM((seq, TOK), F32),
        pltpu.VMEM((seq, 2 * HD), BF16),
        pltpu.VMEM((4, seq, HD), BF16),
        pltpu.VMEM((seq, HD), F32),
        pltpu.VMEM((seq, HD), F32),
        pltpu.VMEM((2, half, TOK), BF16),
        pltpu.VMEM((half, seq), BF16),
        pltpu.VMEM((NX, xrows, 2 * HD), BF16),
        pltpu.VMEM((NX, xrows, 2 * HD), BF16),
        pltpu.VMEM((NX - 1, xrows, 2 * HD), BF16),
        pltpu.VMEM((NX - 1, xrows, 2 * HD), BF16),
        pltpu.VMEM((xrows + 16, 2 * HD), F32),
        pltpu.VMEM((4, zrows, 2 * HD), BF16),
        pltpu.VMEM((NZ, zrows, 2 * HD), BF16),
        dma((7,)),
        dma((8,)), dma((2, CTX)),
        dma((1,)), dma((1,)),
        dma((1,)), dma((1,)),
        dma((1,)), dma((NX,)), dma((NX, 2)), dma((NX,)),
        dma((1,)), dma((NX, 2)),
        dma((1,)), dma((2,)),
        dma((4,)), dma((NZ,)),
    ]
    outs = (
        jax.ShapeDtypeStruct((TOK, width), BF16),
        jax.ShapeDtypeStruct((TOK, key_width), BF16),
        jax.ShapeDtypeStruct((TOK, key_width), BF16),
        jax.ShapeDtypeStruct((frows, 2 * HD), F32),
    )
    parts = pl.pallas_call(
        kernel,
        out_shape=outs,
        in_specs=[any_spec] * 6,
        out_specs=(any_spec, any_spec, any_spec, pl.BlockSpec(memory_space=pltpu.VMEM)),
        scratch_shapes=scratch,
        compiler_params=pltpu.CompilerParams(
            collective_id=0, has_side_effects=True, vmem_limit_bytes=63 << 20
        ),
    )(hidden_in[0], queries[0], key_states[0], value_states[0], out_grad[0], segment_ids)
    dq, dk, dv, dw = pl.pallas_call(
        hand_over,
        out_shape=outs,
        in_specs=[any_spec] * 4,
        out_specs=(any_spec,) * 4,
        scratch_shapes=[pltpu.VMEM(out.shape, out.dtype) for out in outs] + [dma((2, 4))],
    )(*parts)
    return dq[None], dk[None], dv[None], dw


def solution(mesh):
    row = P("dp", "ctx", None)
    return jax.shard_map(
        local,
        mesh=mesh,
        in_specs=(row, row, row, row, row, P("dp", "ctx")),
        out_specs=(row, row, row, P("dp", "ctx")),
        check_vma=False,
    )
```

```python
import functools

import jax
import jax.numpy as jnp
from jax import lax
from jax.experimental import pallas as pl
from jax.experimental.pallas import tpu as pltpu
from jax.sharding import PartitionSpec as P

HD = 128
TOK = 128
CTX = 8
NY = 4
NX = 4
NZ = 4
NC = 2
SPAN = 4
FLOOR = -1e30
SCALE = HD ** (-0.5)
EXP2_SCALE = SCALE * 1.4426950408889634
MESH = pl.DeviceIdType.MESH
F32 = jnp.float32
BF16 = jnp.bfloat16
PEERS = ((1, 2), (0, 2), (1, 1), (1, 3), (0, 1), (0, 3), (1, 0))
ORDER = (1, 2, 3, 0)
NT = (((1,), (1,)), ((), ()))
TN = (((0,), (0,)), ((), ()))


def dot(lhs, rhs, dims=(((1,), (0,)), ((), ()))):
    return lax.dot_general(lhs, rhs, dims, preferred_element_type=F32)


def kernel(
    h, q, k, v, do, seg, dq_out, dk_out, dv_out, w_out,
    hv, qs, dos, ks, vs, segs, segc, dqs, g4, dka, dva, hs, hall,
    csend, crecv, xsend, xrecv, tsum, zsend, zrecv,
    lsem, asend, arecv, osend, orecv, gsend, grecv,
    hsend, harecv, hyrecv, hprecv,
    csem, crsem, xsem, xrsem, zsem, zrsem,
):
    feats = h.shape[1]
    half = feats // 2
    xrows = half // NX
    frows = w_out.shape[0]
    zrows = zsend.shape[1]
    split = (xrows // 2 + 15) // 16 * 16
    dp = lax.axis_index("dp")
    ctx = lax.axis_index("ctx")
    x = dp // (NZ * NC)
    zh = (dp // NC) % NZ
    core = dp % NC
    zl = ctx // NY
    y = ctx % NY
    other = (zl + 1) % 2
    head = 2 * y + zl
    partner = other * NY + y

    def at(place, width):
        return pl.ds(pl.multiple_of(place * width, width), width)

    def place(nx, nz, nc, nl, ny):
        return ((nx * NZ + nz) * NC + nc, nl * NY + ny)

    def remote(src, dst, ssem, rsem, device):
        return pltpu.make_async_remote_copy(
            src_ref=src, dst_ref=dst, send_sem=ssem, recv_sem=rsem,
            device_id=device, device_id_type=MESH,
        )

    def drain(sem, rows, cols):
        whole = hall.at[pl.ds(0, rows), pl.ds(0, cols)]
        pltpu.make_async_copy(whole, whole, sem).wait()

    barrier = pltpu.get_barrier_semaphore()
    count = 0
    for dz in range(NZ):
        for dc in range(NC):
            for dl in range(2):
                if dz + dc + dl:
                    pl.semaphore_signal(
                        barrier, inc=1, device_id_type=MESH,
                        device_id=place(x, (zh + dz) % NZ, (core + dc) % NC, (zl + dl) % 2, y),
                    )
                    count += 1
    for dl in range(2):
        for dy in range(1, NY):
            pl.semaphore_signal(
                barrier, inc=1, device_id_type=MESH,
                device_id=place(x, zh, core, (zl + dl) % 2, (y + dy) % NY),
            )
            count += 1
    for dx in range(1, NX):
        pl.semaphore_signal(
            barrier, inc=1, device_id_type=MESH,
            device_id=place((x + dx) % NX, zh, core, zl, y),
        )
        count += 1

    own = at(ctx, TOK)
    local_in = [
        pltpu.make_async_copy(h, hv, lsem.at[0]),
        pltpu.make_async_copy(q.at[:, at(head, 2 * HD)], qs.at[own, :], lsem.at[1]),
        pltpu.make_async_copy(do.at[:, at(head, 2 * HD)], dos.at[own, :], lsem.at[2]),
        pltpu.make_async_copy(k.at[:, at(head, HD)], ks.at[own, :], lsem.at[3]),
        pltpu.make_async_copy(v.at[:, at(head, HD)], vs.at[own, :], lsem.at[4]),
        pltpu.make_async_copy(seg, segs.at[ctx], lsem.at[5]),
    ]
    for copy in local_in:
        copy.start()
    pl.semaphore_wait(barrier, count)

    def inputs_to(nl, ny, sender, slot=0):
        to_head = 2 * ny + nl
        target = (dp, nl * NY + ny)
        rows = at(sender, TOK)
        pairs = (
            (k.at[:, at(to_head, HD)], ks.at[rows, :]),
            (q.at[:, at(to_head, 2 * HD)], qs.at[rows, :]),
            (v.at[:, at(to_head, HD)], vs.at[rows, :]),
            (do.at[:, at(to_head, 2 * HD)], dos.at[rows, :]),
            (seg, segs.at[sender]),
        )
        return [
            remote(src, dst, asend.at[index // 4 * (1 + slot)], arecv.at[index // 4, sender], target)
            for index, (src, dst) in enumerate(pairs)
        ]

    input_copies = []
    for slot, (dl, dy) in enumerate(PEERS):
        input_copies += inputs_to((zl + dl) % 2, (y + dy) % NY, ctx, slot)
    for copy in input_copies:
        copy.start()

    local_in[0].wait()
    for tile in range(feats // 128):
        turned = jnp.transpose(hv[:, tile * 128 : (tile + 1) * 128])
        row = tile * 128
        while row < (tile + 1) * 128:
            block = row // xrows
            stop = min((block + 1) * xrows, (tile + 1) * 128)
            start = (block // 2) * xrows + row - block * xrows
            hs[block % 2, start : start + stop - row, :] = turned[
                row - tile * 128 : stop - tile * 128, :
            ]
            row = stop

    h_own = pltpu.make_async_copy(hs.at[zl], hall.at[:, own], lsem.at[6])
    h_own.start()

    def x_of(step):
        return (x + ORDER[step]) % NX

    def chunk(step):
        return x_of(step) * xrows

    def h_rows(step, part=None):
        start, size = (0, xrows) if part is None else ((0, split), (split, xrows - split))[part]
        return pl.ds(pl.multiple_of(chunk(step) + start, 16), size)

    def h_across(step, block):
        return remote(
            hs.at[other, h_rows(step), :], hall.at[h_rows(step), at(block, TOK)],
            hsend.at[0], harecv.at[step], (dp, partner),
        )

    def h_block(kind, ny):
        return (zl + kind) % 2 * NY + (ny + NY) % NY

    def h_step(step, kind, way, ny):
        cols = at(h_block(kind, ny), TOK)
        src = hall.at[h_rows(step), cols] if kind else hs.at[zl, h_rows(step), :]
        return remote(
            src, hall.at[h_rows(step), cols], hsend.at[0],
            hyrecv.at[step, kind], (dp, zl * NY + (y + 1 + 2 * way) % NY),
        )

    def h_pass(step, kind, way, ny):
        place_of = hall.at[h_rows(step, way), at(h_block(kind, ny), TOK)]
        return remote(
            place_of, place_of, hsend.at[0],
            hprecv.at[step], (dp, zl * NY + (y + 1 + 2 * way) % NY),
        )

    def h_start(step, kind):
        for way in range(2):
            h_step(step, kind, way, y).start()

    def h_forward(step, kind):
        drain(hyrecv.at[step, kind], xrows, 2 * TOK)
        for way in range(2):
            h_pass(step, kind, way, y - 1 + 2 * way).start()

    def h_arrive(step):
        drain(hprecv.at[step], xrows, 2 * TOK)

    def h_partner(step):
        h_across(step, partner).wait_recv()
        h_start(step, 1)

    h_across(0, ctx).start()
    h_across(1, ctx).start()
    h_start(0, 0)
    h_start(1, 0)

    for copy in local_in[1:]:
        copy.wait()

    def out_refs(block):
        rows = at(block, TOK)
        return (
            (dqs.at[rows, :], dq_out.at[:, at(head, 2 * HD)]),
            (g4.at[zl, rows, :], dk_out.at[:, at(head, HD)]),
            (g4.at[2 + zl, rows, :], dv_out.at[:, at(head, HD)]),
        )

    def trade(block):
        rows = pl.ds(block * TOK, TOK)
        return [
            remote(
                g4.at[2 * kind + zl, rows, :], g4.at[2 * kind + zl, rows, :],
                gsend.at[0], grecv.at[0], (dp, partner),
            )
            for kind in range(2)
        ]

    def finish_keys(block):
        rows = slice(block * TOK, (block + 1) * TOK)
        g4[zl, rows, :] = (dka[rows, :] * SCALE).astype(BF16)
        g4[2 + zl, rows, :] = dva[rows, :].astype(BF16)
        for copy in trade(block):
            copy.start()

    key_iota = lax.broadcasted_iota(jnp.int32, (TOK, 2 * TOK), 0)
    query_iota = lax.broadcasted_iota(jnp.int32, (TOK, 2 * TOK), 1)
    causal = key_iota <= query_iota % TOK

    for block in range(CTX):
        @pl.when(ctx != block)
        def _():
            drain(arecv.at[0, block], 6 * TOK, TOK)
            inputs_to(zl, y, block)[4].wait_recv()

        if block == 1:
            h_across(2, ctx).start()
            h_across(3, ctx).start()
            h_start(2, 0)
            h_start(3, 0)
        if block == 5:
            h_forward(0, 0)
            h_forward(1, 0)
        if block == 6:
            h_partner(0)
            h_partner(1)
        if block == 7:
            h_partner(2)
            h_partner(3)

        first = max(0, block - SPAN)
        rows = slice(block * TOK, (block + 1) * TOK)
        band = slice(first * TOK, (block + 1) * TOK)
        deep = (block - first) * TOK
        seg_row = segs[block].astype(F32)
        segc[rows, :] = jnp.transpose(jnp.broadcast_to(seg_row, (TOK, TOK)))
        seg_row = jnp.concatenate([seg_row, seg_row], axis=1)
        seg_col = segc[band, :]
        seg_col = jnp.concatenate([seg_col, seg_col], axis=1)
        q2 = jnp.concatenate([qs[rows, :HD], qs[rows, HD:]], axis=0)
        do2 = jnp.concatenate([dos[rows, :HD], dos[rows, HD:]], axis=0)
        kw = ks[band, :]
        same = seg_col == seg_row
        scores = dot(kw, q2, NT)
        last = jnp.where(same[deep:] & causal, scores[deep:], FLOOR)
        if deep:
            scores = jnp.concatenate([jnp.where(same[:deep], scores[:deep], FLOOR), last], axis=0)
        else:
            scores = last
        peak = jnp.max(scores, axis=0, keepdims=True)
        weights = jnp.exp2((scores - peak) * EXP2_SCALE)
        probs = weights * (1.0 / jnp.sum(weights, axis=0, keepdims=True))
        probs_b = probs.astype(BF16)
        dprobs = dot(vs[band, :], do2, NT)
        delta = jnp.sum(probs_b.astype(F32) * dprobs, axis=0, keepdims=True)
        dscores = (probs * (dprobs - delta)).astype(BF16)
        dq2 = (dot(dscores, kw, TN) * SCALE).astype(BF16)
        dqs[rows, :HD] = dq2[:TOK]
        dqs[rows, HD:] = dq2[TOK:]
        dk_add = dot(dscores, q2)
        dv_add = dot(probs_b, do2)
        dka[rows, :] = dk_add[deep:]
        dva[rows, :] = dv_add[deep:]
        if deep:
            before = slice(first * TOK, block * TOK)
            dka[before, :] += dk_add[:deep]
            dva[before, :] += dv_add[:deep]
        if block >= SPAN:
            finish_keys(block - SPAN)
    for block in range(CTX - SPAN, CTX):
        finish_keys(block)

    for src, dst in out_refs(ctx):
        pltpu.make_async_copy(src, dst, lsem.at[0]).start()

    def columns(kind):
        return jnp.concatenate([g4[2 * kind], g4[2 * kind + 1]], axis=1)

    far_core = (core + 1) % NC

    def part_rows(part):
        return ((0, split), (split, xrows - split))[part]

    def core_copy(part, step):
        piece = (x_of(step), pl.ds(*part_rows(part)))
        return remote(
            csend.at[piece], crecv.at[piece], csem.at[0], crsem.at[step, part],
            place(x, zh, far_core, zl, y),
        )

    def x_copy(part, step, nx):
        piece = (step, pl.ds(*part_rows(part)))
        return remote(
            xsend.at[piece], xrecv.at[piece], xsem.at[0], xrsem.at[part],
            place(nx, zh, core, zl, y),
        )

    def weights_far(part, step):
        if part == 0:
            h_arrive(step)
        if part == 0 and step == 0:
            h_own.wait()
            drain(grecv.at[0], CTX * TOK, 2 * TOK)
        csend[x_of(step), pl.ds(*part_rows(part)), :] = dot(
            hall[h_rows(step, part), :], columns(far_core)
        ).astype(BF16)
        core_copy(part, step).start()

    def weights_own(part, step):
        rows = pl.ds(*part_rows(part))
        mine = dot(hall[h_rows(step, part), :], columns(core))
        core_copy(part, step).wait_recv()
        total = mine + crecv[x_of(step), rows, :].astype(F32)
        if step < NX - 1:
            xsend[step, rows, :] = total.astype(BF16)
            x_copy(part, step, x_of(step)).start()
        else:
            tsum[rows, :] = total

    def x_finish(part):
        rows = pl.ds(*part_rows(part))
        drain(xrsem.at[part], (NX - 1) * part_rows(part)[1], 2 * HD)
        tsum[rows, :] += (
            xrecv[0, rows, :].astype(F32) + xrecv[1, rows, :].astype(F32)
            + xrecv[2, rows, :].astype(F32)
        )
        for piece in (2 * part, 2 * part + 1):
            zsend[piece] = tsum[piece * frows : piece * frows + zrows, :].astype(BF16)

            @pl.when(z_mine(piece))
            def _():
                z_near(piece).start()

            @pl.when(jnp.logical_not(z_mine(piece)))
            def _():
                z_far(piece).start()

    def z_mine(piece):
        return (2 * zl + piece // 2 == zh) & (piece % 2 == core) & (core == zl)

    def z_far(piece):
        return remote(
            zsend.at[piece], zrecv.at[zh], zsem.at[piece], zrsem.at[zh],
            place(x, 2 * zl + piece // 2, piece % 2, core, y),
        )

    def z_near(piece):
        return pltpu.make_async_copy(zsend.at[piece], zrecv.at[zh], zsem.at[piece])

    def give_back(peers):
        for dl, dy in peers:
            block = (zl + dl) % 2 * NY + (y + dy) % NY
            for src, dst in out_refs(block):
                remote(src, dst, osend.at[0], orecv.at[0], (dp, block)).start()

    tsum[xrows:, :] = jnp.zeros((tsum.shape[0] - xrows, tsum.shape[1]), F32)
    h_forward(2, 0)
    h_forward(3, 0)
    h_forward(0, 1)
    h_forward(1, 1)
    give_back(PEERS[6:])
    h_forward(2, 1)
    weights_far(0, 0)
    h_forward(3, 1)
    weights_far(0, 1)
    weights_own(0, 0)
    give_back(PEERS[:6])
    weights_far(0, 2)
    weights_own(0, 1)
    weights_far(0, 3)
    weights_own(0, 2)
    weights_own(0, 3)
    weights_far(1, 0)
    weights_far(1, 1)
    weights_own(1, 0)
    weights_far(1, 2)
    weights_own(1, 1)
    weights_far(1, 3)
    weights_own(1, 2)
    weights_own(1, 3)

    x_finish(0)
    x_finish(1)

    drain(asend.at[0], half, 4 * TOK)
    for copy in input_copies[4::5]:
        copy.wait_send()
    drain(hsend.at[0], half, 7 * TOK)
    drain(gsend.at[0], CTX * TOK, 2 * TOK)
    drain(csem.at[0], half, 2 * HD)
    drain(xsem.at[0], (NX - 1) * xrows, 2 * HD)
    drain(lsem.at[0], 4 * TOK, TOK)
    drain(osend.at[0], (CTX - 1) * TOK, 4 * TOK)
    drain(orecv.at[0], (CTX - 1) * TOK, 4 * TOK)

    for piece in range(4):
        @pl.when(z_mine(piece))
        def _():
            z_near(piece).wait()

        @pl.when(jnp.logical_not(z_mine(piece)))
        def _():
            z_far(piece).wait_send()

    for sender in range(NZ):
        mine = (sender == zh) & (core == zl) & (zh // 2 == zl)

        @pl.when(jnp.logical_not(mine))
        def _():
            remote(
                zsend.at[0], zrecv.at[sender], zsem.at[0], zrsem.at[sender],
                place(x, zh, core, zl, y),
            ).wait_recv()

    w_out[...] = (
        (zrecv[0, :frows, :].astype(F32) + zrecv[1, :frows, :].astype(F32))
        + (zrecv[2, :frows, :].astype(F32) + zrecv[3, :frows, :].astype(F32))
    )


def hand_over(*refs):
    sources, targets, stages = refs[:4], refs[4:8], refs[8:12]
    sems = refs[12]
    pieces = [
        (index, pl.ds(piece * 32, 32)) for piece in range(TOK // 32) for index in range(3)
    ] + [(3, pl.ds(0, refs[3].shape[0]))]
    loads = [
        pltpu.make_async_copy(
            sources[index].at[rows, :], stages[index].at[rows, :], sems.at[0, number]
        )
        for number, (index, rows) in enumerate(pieces)
    ]
    stores = [
        pltpu.make_async_copy(
            stages[index].at[rows, :], targets[index].at[rows, :], sems.at[1, number]
        )
        for number, (index, rows) in enumerate(pieces)
    ]
    for copy in loads:
        copy.start()
    for load, store in zip(loads, stores):
        load.wait()
        store.start()
    for copy in stores:
        copy.wait()


def local(hidden_in, queries, key_states, value_states, out_grad, segment_ids):
    feats = hidden_in.shape[2]
    width = queries.shape[2]
    key_width = key_states.shape[2]
    half = feats // 2
    xrows = half // NX
    frows = feats // (NX * NZ * NC)
    zrows = -(-frows // 16) * 16
    seq = CTX * TOK
    any_spec = pl.BlockSpec(memory_space=pltpu.HBM)
    dma = pltpu.SemaphoreType.DMA
    scratch = [
        pltpu.VMEM((TOK, feats), BF16),
        pltpu.VMEM((seq, 2 * HD), BF16),
        pltpu.VMEM((seq, 2 * HD), BF16),
        pltpu.VMEM((seq, HD), BF16),
        pltpu.VMEM((seq, HD), BF16),
        pltpu.VMEM((CTX, 1, TOK), jnp.int32),
        pltpu.VMEM((seq, TOK), F32),
        pltpu.VMEM((seq, 2 * HD), BF16),
        pltpu.VMEM((4, seq, HD), BF16),
        pltpu.VMEM((seq, HD), F32),
        pltpu.VMEM((seq, HD), F32),
        pltpu.VMEM((2, half, TOK), BF16),
        pltpu.VMEM((half, seq), BF16),
        pltpu.VMEM((NX, xrows, 2 * HD), BF16),
        pltpu.VMEM((NX, xrows, 2 * HD), BF16),
        pltpu.VMEM((NX - 1, xrows, 2 * HD), BF16),
        pltpu.VMEM((NX - 1, xrows, 2 * HD), BF16),
        pltpu.VMEM((xrows + 16, 2 * HD), F32),
        pltpu.VMEM((4, zrows, 2 * HD), BF16),
        pltpu.VMEM((NZ, zrows, 2 * HD), BF16),
        dma((7,)),
        dma((8,)), dma((2, CTX)),
        dma((1,)), dma((1,)),
        dma((1,)), dma((1,)),
        dma((1,)), dma((NX,)), dma((NX, 2)), dma((NX,)),
        dma((1,)), dma((NX, 2)),
        dma((1,)), dma((2,)),
        dma((4,)), dma((NZ,)),
    ]
    outs = (
        jax.ShapeDtypeStruct((TOK, width), BF16),
        jax.ShapeDtypeStruct((TOK, key_width), BF16),
        jax.ShapeDtypeStruct((TOK, key_width), BF16),
        jax.ShapeDtypeStruct((frows, 2 * HD), F32),
    )
    parts = pl.pallas_call(
        kernel,
        out_shape=outs,
        in_specs=[any_spec] * 6,
        out_specs=(any_spec, any_spec, any_spec, pl.BlockSpec(memory_space=pltpu.VMEM)),
        scratch_shapes=scratch,
        compiler_params=pltpu.CompilerParams(
            collective_id=0, has_side_effects=True, vmem_limit_bytes=63 << 20
        ),
    )(hidden_in[0], queries[0], key_states[0], value_states[0], out_grad[0], segment_ids)
    dq, dk, dv, dw = pl.pallas_call(
        hand_over,
        out_shape=outs,
        in_specs=[any_spec] * 4,
        out_specs=(any_spec,) * 4,
        scratch_shapes=[pltpu.VMEM(out.shape, out.dtype) for out in outs] + [dma((2, 13))],
    )(*parts)
    return dq[None], dk[None], dv[None], dw


def solution(mesh):
    row = P("dp", "ctx", None)
    return jax.shard_map(
        local,
        mesh=mesh,
        in_specs=(row, row, row, row, row, P("dp", "ctx")),
        out_specs=(row, row, row, P("dp", "ctx")),
        check_vma=False,
    )
```

```python
import functools

import jax
import jax.numpy as jnp
from jax import lax
from jax.experimental import pallas as pl
from jax.experimental.pallas import tpu as pltpu
from jax.sharding import PartitionSpec as P

HD = 128
TOK = 128
CTX = 8
NY = 4
NX = 4
NZ = 4
NC = 2
SPAN = 4
FLOOR = -1e30
SCALE = HD ** (-0.5)
EXP2_SCALE = SCALE * 1.4426950408889634
MESH = pl.DeviceIdType.MESH
F32 = jnp.float32
BF16 = jnp.bfloat16
PEERS = ((1, 2), (0, 2), (1, 1), (1, 3), (0, 1), (0, 3), (1, 0))
ORDER = (1, 2, 3, 0)
NT = (((1,), (1,)), ((), ()))
TN = (((0,), (0,)), ((), ()))


def dot(lhs, rhs, dims=(((1,), (0,)), ((), ()))):
    return lax.dot_general(lhs, rhs, dims, preferred_element_type=F32)


def kernel(
    h, q, k, v, do, seg, dq_out, dk_out, dv_out, w_out,
    hv, qs, dos, ks, vs, segs, segc, dqs, g4, dka, dva, hs, hall,
    csend, crecv, xsend, xrecv, tsum, zsend, zrecv,
    lsem, asend, arecv, osend, orecv, gsend, grecv,
    hsend, harecv, hyrecv, hprecv,
    csem, crsem, xsem, xrsem, zsem, zrsem,
):
    feats = h.shape[1]
    half = feats // 2
    xrows = half // NX
    frows = w_out.shape[0]
    zrows = zsend.shape[1]
    split = (xrows // 2 + 15) // 16 * 16
    dp = lax.axis_index("dp")
    ctx = lax.axis_index("ctx")
    x = dp // (NZ * NC)
    zh = (dp // NC) % NZ
    core = dp % NC
    zl = ctx // NY
    y = ctx % NY
    other = (zl + 1) % 2
    head = 2 * y + zl
    partner = other * NY + y

    def at(place, width):
        return pl.ds(pl.multiple_of(place * width, width), width)

    def place(nx, nz, nc, nl, ny):
        return ((nx * NZ + nz) * NC + nc, nl * NY + ny)

    def remote(src, dst, ssem, rsem, device):
        return pltpu.make_async_remote_copy(
            src_ref=src, dst_ref=dst, send_sem=ssem, recv_sem=rsem,
            device_id=device, device_id_type=MESH,
        )

    def drain(sem, rows, cols):
        whole = hall.at[pl.ds(0, rows), pl.ds(0, cols)]
        pltpu.make_async_copy(whole, whole, sem).wait()

    barrier = pltpu.get_barrier_semaphore()
    count = 0
    for dz in range(NZ):
        for dc in range(NC):
            for dl in range(2):
                if dz + dc + dl:
                    pl.semaphore_signal(
                        barrier, inc=1, device_id_type=MESH,
                        device_id=place(x, (zh + dz) % NZ, (core + dc) % NC, (zl + dl) % 2, y),
                    )
                    count += 1
    for dl in range(2):
        for dy in range(1, NY):
            pl.semaphore_signal(
                barrier, inc=1, device_id_type=MESH,
                device_id=place(x, zh, core, (zl + dl) % 2, (y + dy) % NY),
            )
            count += 1
    for dx in range(1, NX):
        pl.semaphore_signal(
            barrier, inc=1, device_id_type=MESH,
            device_id=place((x + dx) % NX, zh, core, zl, y),
        )
        count += 1

    own = at(ctx, TOK)
    local_in = [
        pltpu.make_async_copy(h, hv, lsem.at[0]),
        pltpu.make_async_copy(q.at[:, at(head, 2 * HD)], qs.at[own, :], lsem.at[1]),
        pltpu.make_async_copy(do.at[:, at(head, 2 * HD)], dos.at[own, :], lsem.at[2]),
        pltpu.make_async_copy(k.at[:, at(head, HD)], ks.at[own, :], lsem.at[3]),
        pltpu.make_async_copy(v.at[:, at(head, HD)], vs.at[own, :], lsem.at[4]),
        pltpu.make_async_copy(seg, segs.at[ctx], lsem.at[5]),
    ]
    for copy in local_in:
        copy.start()
    pl.semaphore_wait(barrier, count)

    def inputs_to(nl, ny, sender, slot=0):
        to_head = 2 * ny + nl
        target = (dp, nl * NY + ny)
        rows = at(sender, TOK)
        pairs = (
            (k.at[:, at(to_head, HD)], ks.at[rows, :]),
            (q.at[:, at(to_head, 2 * HD)], qs.at[rows, :]),
            (v.at[:, at(to_head, HD)], vs.at[rows, :]),
            (do.at[:, at(to_head, 2 * HD)], dos.at[rows, :]),
            (seg, segs.at[sender]),
        )
        return [
            remote(src, dst, asend.at[index // 4 * (1 + slot)], arecv.at[index // 4, sender], target)
            for index, (src, dst) in enumerate(pairs)
        ]

    input_copies = []
    for slot, (dl, dy) in enumerate(PEERS):
        input_copies += inputs_to((zl + dl) % 2, (y + dy) % NY, ctx, slot)
    for copy in input_copies:
        copy.start()

    local_in[0].wait()
    for tile in range(feats // 128):
        turned = jnp.transpose(hv[:, tile * 128 : (tile + 1) * 128])
        row = tile * 128
        while row < (tile + 1) * 128:
            block = row // xrows
            stop = min((block + 1) * xrows, (tile + 1) * 128)
            start = (block // 2) * xrows + row - block * xrows
            hs[block % 2, start : start + stop - row, :] = turned[
                row - tile * 128 : stop - tile * 128, :
            ]
            row = stop

    h_own = pltpu.make_async_copy(hs.at[zl], hall.at[:, own], lsem.at[6])
    h_own.start()

    def x_of(step):
        return (x + ORDER[step]) % NX

    def chunk(step):
        return x_of(step) * xrows

    def h_rows(step, part=None):
        start, size = (0, xrows) if part is None else ((0, split), (split, xrows - split))[part]
        return pl.ds(pl.multiple_of(chunk(step) + start, 16), size)

    def h_across(step, block):
        return remote(
            hs.at[other, h_rows(step), :], hall.at[h_rows(step), at(block, TOK)],
            hsend.at[0], harecv.at[step], (dp, partner),
        )

    def h_block(kind, ny):
        return (zl + kind) % 2 * NY + (ny + NY) % NY

    def h_step(step, kind, way, ny):
        cols = at(h_block(kind, ny), TOK)
        src = hall.at[h_rows(step), cols] if kind else hs.at[zl, h_rows(step), :]
        return remote(
            src, hall.at[h_rows(step), cols], hsend.at[0],
            hyrecv.at[step, kind], (dp, zl * NY + (y + 1 + 2 * way) % NY),
        )

    def h_pass(step, kind, way, ny):
        place_of = hall.at[h_rows(step, way), at(h_block(kind, ny), TOK)]
        return remote(
            place_of, place_of, hsend.at[0],
            hprecv.at[step], (dp, zl * NY + (y + 1 + 2 * way) % NY),
        )

    def h_start(step, kind):
        for way in range(2):
            h_step(step, kind, way, y).start()

    def h_forward(step, kind):
        drain(hyrecv.at[step, kind], xrows, 2 * TOK)
        for way in range(2):
            h_pass(step, kind, way, y - 1 + 2 * way).start()

    def h_arrive(step):
        drain(hprecv.at[step], xrows, 2 * TOK)

    def h_partner(step):
        h_across(step, partner).wait_recv()
        h_start(step, 1)

    h_across(0, ctx).start()
    h_across(1, ctx).start()
    h_start(0, 0)
    h_start(1, 0)

    for copy in local_in[1:]:
        copy.wait()

    def out_refs(block):
        rows = at(block, TOK)
        return (
            (dqs.at[rows, :], dq_out.at[:, at(head, 2 * HD)]),
            (g4.at[zl, rows, :], dk_out.at[:, at(head, HD)]),
            (g4.at[2 + zl, rows, :], dv_out.at[:, at(head, HD)]),
        )

    def trade(block):
        rows = pl.ds(block * TOK, TOK)
        return [
            remote(
                g4.at[2 * kind + zl, rows, :], g4.at[2 * kind + zl, rows, :],
                gsend.at[0], grecv.at[0], (dp, partner),
            )
            for kind in range(2)
        ]

    def finish_keys(block):
        rows = slice(block * TOK, (block + 1) * TOK)
        g4[zl, rows, :] = (dka[rows, :] * SCALE).astype(BF16)
        g4[2 + zl, rows, :] = dva[rows, :].astype(BF16)
        for copy in trade(block):
            copy.start()

    key_iota = lax.broadcasted_iota(jnp.int32, (TOK, 2 * TOK), 0)
    query_iota = lax.broadcasted_iota(jnp.int32, (TOK, 2 * TOK), 1)
    causal = key_iota <= query_iota % TOK

    for block in range(CTX):
        @pl.when(ctx != block)
        def _():
            drain(arecv.at[0, block], 6 * TOK, TOK)
            inputs_to(zl, y, block)[4].wait_recv()

        if block == 1:
            h_across(2, ctx).start()
            h_across(3, ctx).start()
            h_start(2, 0)
            h_start(3, 0)
        if block == 5:
            h_forward(0, 0)
            h_forward(1, 0)
        if block == 6:
            h_partner(0)
            h_partner(1)
        if block == 7:
            h_partner(2)
            h_partner(3)

        first = max(0, block - SPAN)
        rows = slice(block * TOK, (block + 1) * TOK)
        band = slice(first * TOK, (block + 1) * TOK)
        deep = (block - first) * TOK
        seg_row = segs[block].astype(F32)
        segc[rows, :] = jnp.transpose(jnp.broadcast_to(seg_row, (TOK, TOK)))
        seg_row = jnp.concatenate([seg_row, seg_row], axis=1)
        seg_col = segc[band, :]
        seg_col = jnp.concatenate([seg_col, seg_col], axis=1)
        q2 = jnp.concatenate([qs[rows, :HD], qs[rows, HD:]], axis=0)
        do2 = jnp.concatenate([dos[rows, :HD], dos[rows, HD:]], axis=0)
        kw = ks[band, :]
        same = seg_col == seg_row
        scores = dot(kw, q2, NT)
        last = jnp.where(same[deep:] & causal, scores[deep:], FLOOR)
        if deep:
            scores = jnp.concatenate([jnp.where(same[:deep], scores[:deep], FLOOR), last], axis=0)
        else:
            scores = last
        peak = jnp.max(scores, axis=0, keepdims=True)
        weights = jnp.exp2((scores - peak) * EXP2_SCALE)
        probs = weights * (1.0 / jnp.sum(weights, axis=0, keepdims=True))
        probs_b = probs.astype(BF16)
        dprobs = dot(vs[band, :], do2, NT)
        delta = jnp.sum(probs_b.astype(F32) * dprobs, axis=0, keepdims=True)
        dscores = (probs * (dprobs - delta)).astype(BF16)
        dq2 = (dot(dscores, kw, TN) * SCALE).astype(BF16)
        dqs[rows, :HD] = dq2[:TOK]
        dqs[rows, HD:] = dq2[TOK:]
        dk_add = dot(dscores, q2)
        dv_add = dot(probs_b, do2)
        dka[rows, :] = dk_add[deep:]
        dva[rows, :] = dv_add[deep:]
        if deep:
            before = slice(first * TOK, block * TOK)
            dka[before, :] += dk_add[:deep]
            dva[before, :] += dv_add[:deep]
        if block >= SPAN:
            finish_keys(block - SPAN)
    for block in range(CTX - SPAN, CTX):
        finish_keys(block)

    for src, dst in out_refs(ctx):
        pltpu.make_async_copy(src, dst, lsem.at[0]).start()

    def columns(kind):
        return jnp.concatenate([g4[2 * kind], g4[2 * kind + 1]], axis=1)

    far_core = (core + 1) % NC

    def part_rows(part):
        return ((0, split), (split, xrows - split))[part]

    def core_copy(part, step):
        piece = (x_of(step), pl.ds(*part_rows(part)))
        return remote(
            csend.at[piece], crecv.at[piece], csem.at[0], crsem.at[step, part],
            place(x, zh, far_core, zl, y),
        )

    def x_copy(part, step, nx):
        piece = (step, pl.ds(*part_rows(part)))
        return remote(
            xsend.at[piece], xrecv.at[piece], xsem.at[0], xrsem.at[part],
            place(nx, zh, core, zl, y),
        )

    def weights_far(part, step):
        if part == 0:
            h_arrive(step)
        if part == 0 and step == 0:
            h_own.wait()
            drain(grecv.at[0], CTX * TOK, 2 * TOK)
        csend[x_of(step), pl.ds(*part_rows(part)), :] = dot(
            hall[h_rows(step, part), :], columns(far_core)
        ).astype(BF16)
        core_copy(part, step).start()

    def weights_own(part, step):
        rows = pl.ds(*part_rows(part))
        mine = dot(hall[h_rows(step, part), :], columns(core))
        core_copy(part, step).wait_recv()
        total = mine + crecv[x_of(step), rows, :].astype(F32)
        if step < NX - 1:
            xsend[step, rows, :] = total.astype(BF16)
            x_copy(part, step, x_of(step)).start()
        else:
            tsum[rows, :] = total

    def x_finish(part):
        rows = pl.ds(*part_rows(part))
        drain(xrsem.at[part], (NX - 1) * part_rows(part)[1], 2 * HD)
        tsum[rows, :] += (
            xrecv[0, rows, :].astype(F32) + xrecv[1, rows, :].astype(F32)
            + xrecv[2, rows, :].astype(F32)
        )
        for piece in (2 * part, 2 * part + 1):
            zsend[piece] = tsum[piece * frows : piece * frows + zrows, :].astype(BF16)

            @pl.when(z_mine(piece))
            def _():
                z_near(piece).start()

            @pl.when(jnp.logical_not(z_mine(piece)))
            def _():
                z_far(piece).start()

    def z_mine(piece):
        return (2 * zl + piece // 2 == zh) & (piece % 2 == core) & (core == zl)

    def z_far(piece):
        return remote(
            zsend.at[piece], zrecv.at[zh], zsem.at[piece], zrsem.at[zh],
            place(x, 2 * zl + piece // 2, piece % 2, core, y),
        )

    def z_near(piece):
        return pltpu.make_async_copy(zsend.at[piece], zrecv.at[zh], zsem.at[piece])

    def give_back(peers):
        for dl, dy in peers:
            block = (zl + dl) % 2 * NY + (y + dy) % NY
            for src, dst in out_refs(block):
                remote(src, dst, osend.at[0], orecv.at[0], (dp, block)).start()

    tsum[xrows:, :] = jnp.zeros((tsum.shape[0] - xrows, tsum.shape[1]), F32)
    h_forward(2, 0)
    h_forward(3, 0)
    h_forward(0, 1)
    h_forward(1, 1)
    give_back(PEERS[6:])
    h_forward(2, 1)
    weights_far(0, 0)
    h_forward(3, 1)
    weights_far(0, 1)
    weights_own(0, 0)
    give_back(PEERS[:3])
    weights_far(0, 2)
    weights_own(0, 1)
    weights_far(0, 3)
    weights_own(0, 2)
    give_back(PEERS[3:6])
    weights_own(0, 3)
    weights_far(1, 0)
    weights_far(1, 1)
    weights_own(1, 0)
    weights_far(1, 2)
    weights_own(1, 1)
    weights_far(1, 3)
    weights_own(1, 2)
    weights_own(1, 3)

    x_finish(0)
    x_finish(1)

    drain(asend.at[0], half, 4 * TOK)
    for copy in input_copies[4::5]:
        copy.wait_send()
    drain(hsend.at[0], half, 7 * TOK)
    drain(gsend.at[0], CTX * TOK, 2 * TOK)
    drain(csem.at[0], half, 2 * HD)
    drain(xsem.at[0], (NX - 1) * xrows, 2 * HD)
    drain(lsem.at[0], 4 * TOK, TOK)
    drain(osend.at[0], (CTX - 1) * TOK, 4 * TOK)
    drain(orecv.at[0], (CTX - 1) * TOK, 4 * TOK)

    for piece in range(4):
        @pl.when(z_mine(piece))
        def _():
            z_near(piece).wait()

        @pl.when(jnp.logical_not(z_mine(piece)))
        def _():
            z_far(piece).wait_send()

    for sender in range(NZ):
        mine = (sender == zh) & (core == zl) & (zh // 2 == zl)

        @pl.when(jnp.logical_not(mine))
        def _():
            remote(
                zsend.at[0], zrecv.at[sender], zsem.at[0], zrsem.at[sender],
                place(x, zh, core, zl, y),
            ).wait_recv()

    w_out[...] = (
        (zrecv[0, :frows, :].astype(F32) + zrecv[1, :frows, :].astype(F32))
        + (zrecv[2, :frows, :].astype(F32) + zrecv[3, :frows, :].astype(F32))
    )


def hand_over(*refs):
    sources, targets, stages = refs[:4], refs[4:8], refs[8:12]
    sems = refs[12]
    pieces = [
        (index, pl.ds(piece * 32, 32)) for piece in range(TOK // 32) for index in range(3)
    ] + [(3, pl.ds(0, refs[3].shape[0]))]
    loads = [
        pltpu.make_async_copy(
            sources[index].at[rows, :], stages[index].at[rows, :], sems.at[0, number]
        )
        for number, (index, rows) in enumerate(pieces)
    ]
    stores = [
        pltpu.make_async_copy(
            stages[index].at[rows, :], targets[index].at[rows, :], sems.at[1, number]
        )
        for number, (index, rows) in enumerate(pieces)
    ]
    for copy in loads:
        copy.start()
    for load, store in zip(loads, stores):
        load.wait()
        store.start()
    for copy in stores:
        copy.wait()


def local(hidden_in, queries, key_states, value_states, out_grad, segment_ids):
    feats = hidden_in.shape[2]
    width = queries.shape[2]
    key_width = key_states.shape[2]
    half = feats // 2
    xrows = half // NX
    frows = feats // (NX * NZ * NC)
    zrows = -(-frows // 16) * 16
    seq = CTX * TOK
    any_spec = pl.BlockSpec(memory_space=pltpu.HBM)
    dma = pltpu.SemaphoreType.DMA
    scratch = [
        pltpu.VMEM((TOK, feats), BF16),
        pltpu.VMEM((seq, 2 * HD), BF16),
        pltpu.VMEM((seq, 2 * HD), BF16),
        pltpu.VMEM((seq, HD), BF16),
        pltpu.VMEM((seq, HD), BF16),
        pltpu.VMEM((CTX, 1, TOK), jnp.int32),
        pltpu.VMEM((seq, TOK), F32),
        pltpu.VMEM((seq, 2 * HD), BF16),
        pltpu.VMEM((4, seq, HD), BF16),
        pltpu.VMEM((seq, HD), F32),
        pltpu.VMEM((seq, HD), F32),
        pltpu.VMEM((2, half, TOK), BF16),
        pltpu.VMEM((half, seq), BF16),
        pltpu.VMEM((NX, xrows, 2 * HD), BF16),
        pltpu.VMEM((NX, xrows, 2 * HD), BF16),
        pltpu.VMEM((NX - 1, xrows, 2 * HD), BF16),
        pltpu.VMEM((NX - 1, xrows, 2 * HD), BF16),
        pltpu.VMEM((xrows + 16, 2 * HD), F32),
        pltpu.VMEM((4, zrows, 2 * HD), BF16),
        pltpu.VMEM((NZ, zrows, 2 * HD), BF16),
        dma((7,)),
        dma((8,)), dma((2, CTX)),
        dma((1,)), dma((1,)),
        dma((1,)), dma((1,)),
        dma((1,)), dma((NX,)), dma((NX, 2)), dma((NX,)),
        dma((1,)), dma((NX, 2)),
        dma((1,)), dma((2,)),
        dma((4,)), dma((NZ,)),
    ]
    outs = (
        jax.ShapeDtypeStruct((TOK, width), BF16),
        jax.ShapeDtypeStruct((TOK, key_width), BF16),
        jax.ShapeDtypeStruct((TOK, key_width), BF16),
        jax.ShapeDtypeStruct((frows, 2 * HD), F32),
    )
    parts = pl.pallas_call(
        kernel,
        out_shape=outs,
        in_specs=[any_spec] * 6,
        out_specs=(any_spec, any_spec, any_spec, pl.BlockSpec(memory_space=pltpu.VMEM)),
        scratch_shapes=scratch,
        compiler_params=pltpu.CompilerParams(
            collective_id=0, has_side_effects=True, vmem_limit_bytes=63 << 20
        ),
    )(hidden_in[0], queries[0], key_states[0], value_states[0], out_grad[0], segment_ids)
    dq, dk, dv, dw = pl.pallas_call(
        hand_over,
        out_shape=outs,
        in_specs=[any_spec] * 4,
        out_specs=(any_spec,) * 4,
        scratch_shapes=[pltpu.VMEM(out.shape, out.dtype) for out in outs] + [dma((2, 13))],
    )(*parts)
    return dq[None], dk[None], dv[None], dw


def solution(mesh):
    row = P("dp", "ctx", None)
    return jax.shard_map(
        local,
        mesh=mesh,
        in_specs=(row, row, row, row, row, P("dp", "ctx")),
        out_specs=(row, row, row, P("dp", "ctx")),
        check_vma=False,
    )
```
